256 devices in a mesh: seq: 32 (over x_hi, z, core), tp: 8 (over y, x_lo).
Axes of the slice: x: 4 (x_hi: 2, x_lo: 2; x = x_hi * 2 + x_lo), y: 4, z: 8, core: 2. Of those that a mesh axis runs over, the one named last changes fastest.
Arguments:
- queries: bfloat16 [8, 4096, 4096], P('tp', 'seq'), may hold values from -9 to 9
- key_rows: bfloat16 [8, 4096, 4096], P('tp', 'seq'), may hold values from -6 to 6
- values: bfloat16 [8, 4096, 4096], P('tp', 'seq'), may hold values from -6 to 6
- upstream: bfloat16 [8, 4096, 4096], P(None, 'seq', 'tp'), may hold values from -6 to 6
- out_weight: bfloat16 [4096, 4096], P(None, 'tp'), may hold values from -0.09375 to 0.09375
- blocks: int32 [64, 4], replicated, may hold values from 0 to 63, as said below
Outputs:
- attended: bfloat16 [8, 4096, 4096], P('tp', 'seq')
- grad_queries: bfloat16 [8, 4096, 4096], P('tp', 'seq')
- grad_keys: bfloat16 [8, 4096, 4096], P('tp', 'seq')
- grad_values: bfloat16 [8, 4096, 4096], P('tp', 'seq')
- grad_weight: float32 [4096, 4096], P('seq', 'tp')
The draws below stay inside these ranges and needn't reach their ends.
Inputs may be any that keep to these rules, and one draw needn't show every extreme that they name: Row a lists the blocks a - 1, a and a + 1 modulo 64, then one block 2 to 62 blocks after a modulo 64; no row names a block twice.
All inputs are finite; a program needn't handle non-finite values.
Results may differ from the reference program's by a relative error of at most 0.022.
Values may be sent and summed in bfloat16 or wider, within the bound.
A program may use at most 128 MiB of HBM per device.

```python
import math
import jax
import jax.numpy as jnp
from jax import lax

D = 4096
HEADS = 32
HD = 128
BLK = 64
NB = 4
SEQS = 8
LEN = 4096
N_TP = 8


def draw_queries(key, part):
    own_key = jax.random.fold_in(key, 1)
    return jnp.clip(jax.random.normal(own_key, (SEQS, LEN, D), jnp.float32), -6.0, 6.0).astype(jnp.bfloat16)


def draw_key_rows(key, part):
    own_key = jax.random.fold_in(key, 2)
    return jnp.clip(jax.random.normal(own_key, (SEQS, LEN, D), jnp.float32), -6.0, 6.0).astype(jnp.bfloat16)


def draw_blocks(key, part):
    block_total = LEN // BLK
    places = jnp.arange(block_total, dtype=jnp.int32)
    jitter = jax.random.randint(key, (block_total,), 0, block_total - 3, dtype=jnp.int32)
    window = jnp.stack([places - 1, places, places + 1], axis=1) % block_total
    distant = ((places + 2 + jitter) % block_total)[:, None]
    return jnp.concatenate([window, distant], axis=1).astype(jnp.int32)


def with_spikes(result, key, source, target, blocks, factor):
    def block_of(axis_at):
        return (jnp.arange(result.shape[axis_at]) // (result.shape[axis_at] // blocks)).reshape((-1,) + (1,) * (result.ndim - 1 - axis_at))

    one_side = jax.random.permutation(key, blocks)[block_of(target)]
    far = (block_of(target) + blocks // 2) % blocks
    return jnp.where((block_of(source) == one_side) | (block_of(source) == far), factor * result, result)


def levels(key, dims, pieces, smallest, high):
    def one(dim, parts):
        steps = jax.random.uniform(jax.random.fold_in(jax.random.fold_in(key, 6), dim), (parts,), jnp.float32, smallest / len(pieces), high / len(pieces))
        return jnp.repeat(jnp.exp(steps), dims[dim] // parts).reshape((-1,) + (1,) * (len(dims) - dim - 1))

    factor_of = one(*pieces[0])
    for cut in pieces[1:]:
        factor_of = factor_of * one(*cut)
    return factor_of


def bell_draw(rng, dims, scale, most, cuts=(), held_as=jnp.bfloat16):
    entries = scale * jax.random.normal(rng, dims, jnp.float32)
    if cuts:
        entries = entries * levels(rng, dims, cuts, -0.22, 0.18)
    return jnp.clip(entries, -most, most).astype(held_as)


def heavy_noise(stream_key, shape, deviation, reach, cuts, heavy, held_as=jnp.bfloat16):
    drawn = deviation * jax.random.normal(stream_key, shape, jnp.float32)
    if cuts:
        drawn = drawn * levels(stream_key, shape, cuts, -0.22, 0.18)
    return jnp.clip(with_spikes(drawn, jax.random.fold_in(stream_key, 3), *heavy), -reach, reach).astype(held_as)


def setup_inputs(seed: int = 0) -> dict:
    keys = jax.random.split(jax.random.key(seed), 7)
    queries = draw_queries(jax.random.fold_in(keys[6], 71), 0)
    key_rows = draw_key_rows(jax.random.fold_in(keys[6], 71), 0)
    values = bell_draw(keys[2], (SEQS, LEN, D), 1.0, 6.0, ((0, 8), (1, 32)))
    upstream = heavy_noise(keys[3], (SEQS, LEN, D), 1.0, 6.0, ((1, 32), (2, 8)), (2, 0, 8, 2.0))
    out_weight = bell_draw(keys[4], (D, D), D ** -0.5, 0.09375, ((1, 8),))
    blocks = draw_blocks(jax.random.fold_in(keys[6], 71), 0)
    return {"queries": queries, "key_rows": key_rows, "values": values, "upstream": upstream, "out_weight": out_weight, "blocks": blocks}


def head_pass(query_rows, key_rows, value_rows, grad_rows, blocks):
    block_count = blocks.shape[0]
    factor = 1.0 / math.sqrt(HD)
    query_tiles = query_rows.reshape(block_count, BLK, HD).astype(jnp.float32)
    key_tiles = key_rows.reshape(block_count, BLK, HD).astype(jnp.float32)
    value_tiles = value_rows.reshape(block_count, BLK, HD).astype(jnp.float32)
    grad_tiles = grad_rows.reshape(block_count, BLK, HD).astype(jnp.float32)
    key_set = key_tiles[blocks].reshape(block_count, NB * BLK, HD)
    value_set = value_tiles[blocks].reshape(block_count, NB * BLK, HD)
    scores = jnp.einsum('qid,qjd->qij', query_tiles, key_set) * factor
    row_max = lax.optimization_barrier(jnp.max(scores, axis=-1, keepdims=True))
    shifted = jnp.exp(scores - row_max)
    soft_probs = shifted / lax.optimization_barrier(jnp.sum(shifted, axis=-1, keepdims=True))
    probs_low = lax.optimization_barrier(soft_probs.astype(jnp.bfloat16)).astype(jnp.float32)
    context = lax.optimization_barrier(jnp.einsum('qij,qjd->qid', probs_low, value_set).astype(jnp.bfloat16))
    row_delta = lax.optimization_barrier(jnp.sum(grad_tiles * context.astype(jnp.float32), axis=-1, keepdims=True))
    dprobs = jnp.einsum('qid,qjd->qij', grad_tiles, value_set)
    dscores = lax.optimization_barrier((soft_probs * (dprobs - row_delta) * factor).astype(jnp.bfloat16)).astype(jnp.float32)
    query_grad = jnp.einsum('qij,qjd->qid', dscores, key_set).astype(jnp.bfloat16)
    flat_list = blocks.reshape(-1)
    key_parts = jnp.einsum('qij,qid->qjd', dscores, query_tiles).reshape(block_count * NB, BLK, HD)
    value_parts = jnp.einsum('qij,qid->qjd', probs_low, grad_tiles).reshape(block_count * NB, BLK, HD)
    key_grad = jnp.zeros((block_count, BLK, HD), jnp.float32).at[flat_list].add(key_parts).astype(jnp.bfloat16)
    value_grad = jnp.zeros((block_count, BLK, HD), jnp.float32).at[flat_list].add(value_parts).astype(jnp.bfloat16)
    length = block_count * BLK
    return (context.reshape(length, HD), query_grad.reshape(length, HD), key_grad.reshape(length, HD), value_grad.reshape(length, HD))

def reference(queries, key_rows, values, upstream, out_weight, blocks):
    col_width = D // N_TP

    def add_block(running, column_block):
        start_col = (column_block * col_width).astype(jnp.int32)
        grad_part = lax.dynamic_slice_in_dim(upstream, start_col, col_width, 2).astype(jnp.float32)
        weight_part = lax.dynamic_slice_in_dim(out_weight, start_col, col_width, 1).astype(jnp.float32)
        block_term = jnp.einsum('stc,dc->std', grad_part, weight_part)
        rounded = lax.optimization_barrier(block_term.astype(jnp.bfloat16)).astype(jnp.float32)
        return (running + rounded, None)
    summed, unused = lax.scan(add_block, jnp.zeros((SEQS, LEN, D), jnp.float32), jnp.arange(N_TP, dtype=jnp.int32))
    grad_out = summed.astype(jnp.bfloat16)

    def by_heads(array):
        return array.reshape(SEQS, LEN, HEADS, HD).transpose(0, 2, 1, 3).reshape(SEQS * HEADS, LEN, HD)

    def from_heads(array):
        return array.reshape(SEQS, HEADS, LEN, HD).transpose(0, 2, 1, 3).reshape(SEQS, LEN, D)

    def one_head(packed):
        return head_pass(packed[0], packed[1], packed[2], packed[3], blocks)
    context, query_grad, key_grad, value_grad = lax.map(one_head, (by_heads(queries), by_heads(key_rows), by_heads(values), by_heads(grad_out)))
    attended = from_heads(context)
    grad_weight = jnp.dot(attended.reshape(SEQS * LEN, D).T, upstream.reshape(SEQS * LEN, D), preferred_element_type=jnp.float32)
    return (attended, from_heads(query_grad), from_heads(key_grad), from_heads(value_grad), grad_weight)
```

```python
import functools
import math

import jax
import jax.numpy as jnp
from jax import lax
from jax.experimental import pallas as pl
from jax.experimental.pallas import tpu as pltpu
from jax.sharding import PartitionSpec as P

HD = 128
BLK = 64
NB = 4
MESH = pl.DeviceIdType.MESH
BF16 = jnp.bfloat16
F32 = jnp.float32

NZ = 8
NY = 4
NSEQ = 32
ROWS = 128
WIDE = 512
D = 4096


def seq_of(x_hi, z, core):
    return x_hi * 16 + z * 2 + core


def near_far(step, place, count):
    half = (step + 1) // 2
    return lax.rem(jnp.where(lax.rem(step, 2) == 1, place + half, place + count - half), count)


def seq_peer(step, me):
    z = near_far(step // 4, lax.rem(me // 2, NZ), NZ)
    x_hi = lax.rem(me // 16 + lax.rem(step, 2), 2)
    core = lax.rem(lax.rem(me, 2) + lax.rem(step // 2, 2), 2)
    return seq_of(x_hi, z, core)


def col(index):
    return pl.ds(pl.multiple_of(index * HD, HD), HD)


def row(index, size=ROWS):
    return pl.ds(pl.multiple_of(index * size, size), size)


def chunk_at(step, z):
    return near_far(NZ - 1 - step, z, NZ)


def enter(me, tp):
    barrier = pltpu.get_barrier_semaphore()

    def greet_seq(d, carry):
        pl.semaphore_signal(
            barrier, inc=1, device_id=(lax.rem(me + d, NSEQ), tp), device_id_type=MESH
        )
        return carry

    def greet_tp(d, carry):
        pl.semaphore_signal(
            barrier, inc=1, device_id=(me, lax.rem(tp + d, 8)), device_id_type=MESH
        )
        return carry

    lax.fori_loop(1, NSEQ, greet_seq, 0)
    lax.fori_loop(1, 8, greet_tp, 0)
    pl.semaphore_wait(barrier, NSEQ - 1 + 7)


def gather_in_kernel(
    q_ref, k_ref, v_ref, u_ref, w_ref,
    qh_ref, kh_ref, vh_ref, gh_ref,
    u_buf, w_buf, terms, y_got, keep, x_send, x_got, g_send,
    load_sem, own_sem, send_sem, recv_sem, y_send_sem, y_recv_sem, x_send_sem, x_recv_sem,
    g_send_sem, g_recv_sem, g_own_sem,
):
    me = lax.axis_index("seq")
    tp = lax.axis_index("tp")
    z = lax.rem(me // 2, NZ)
    y, x_lo = tp // 2, lax.rem(tp, 2)
    load_u = pltpu.make_async_copy(u_ref, u_buf, load_sem.at[0])
    load_w = pltpu.make_async_copy(w_ref, w_buf, load_sem.at[1])
    load_u.start()
    load_w.start()
    enter(me, tp)

    sources = (q_ref, k_ref, v_ref)
    targets = (qh_ref, kh_ref, vh_ref)
    for a in range(3):
        pltpu.make_async_copy(
            sources[a].at[:, col(me)], targets[a].at[row(me), :], own_sem.at[a]
        ).start()

        def send_heads(step, carry, a=a):
            peer = seq_peer(step, me)
            pltpu.make_async_remote_copy(
                src_ref=sources[a].at[:, col(peer)],
                dst_ref=targets[a].at[row(me), :],
                send_sem=send_sem.at[a],
                recv_sem=recv_sem.at[a],
                device_id=(peer, tp),
                device_id_type=MESH,
            ).start()
            return carry

        lax.fori_loop(1, NSEQ, send_heads, 0)

    load_u.wait()
    load_w.wait()

    def y_copy(j, d):
        other = lax.rem(y + d, NY)
        return pltpu.make_async_remote_copy(
            src_ref=terms.at[j, row(other, 256), :],
            dst_ref=y_got.at[j, d - 1],
            send_sem=y_send_sem.at[j, d - 1],
            recv_sem=y_recv_sem.at[j, d - 1],
            device_id=(me, other * 2 + x_lo),
            device_id_type=MESH,
        )

    def x_copy(j):
        return pltpu.make_async_remote_copy(
            src_ref=x_send.at[j],
            dst_ref=x_got.at[j],
            send_sem=x_send_sem.at[j],
            recv_sem=x_recv_sem.at[j],
            device_id=(me, y * 2 + 1 - x_lo),
            device_id_type=MESH,
        )

    def stage_terms(j):
        chunk = chunk_at(j, z)
        for part in range(2):
            rows = pl.ds(pl.multiple_of(part * 2048 + chunk * 256, 256), 256)
            terms[j, :, part * 256 : (part + 1) * 256] = lax.dot_general(
                u_buf[...], w_buf[rows, :], (((1,), (1,)), ((), ())), preferred_element_type=F32
            ).astype(BF16)
        for d in (2, 1, 3):
            y_copy(j, d).start()

    def stage_y(j):
        for d in (1, 2, 3):
            y_copy(j, d).wait_recv()

        def total(x):
            rows = pl.ds(pl.multiple_of(y * 256 + x * 128, 128), 128)
            here = pl.ds(pl.multiple_of(x * 128, 128), 128)
            result = terms[j, rows, :].astype(F32)
            for d in range(3):
                result = result + y_got[j, d, here, :].astype(F32)
            return result

        x_send[j] = total(1 - x_lo).astype(BF16)
        x_copy(j).start()
        keep[j] = total(x_lo)

    def stage_x(j):
        x_copy(j).wait_recv()
        g_send[j] = (keep[j] + x_got[j].astype(F32)).astype(BF16)
        chunk = chunk_at(j, z)
        for part in range(4):
            peer = seq_of(part // 2, chunk, part % 2)
            source = g_send.at[j, :, part * HD : (part + 1) * HD]
            target = gh_ref.at[row(me), :]

            @pl.when(peer == me)
            def _():
                pltpu.make_async_copy(source, target, g_own_sem).start()

            @pl.when(peer != me)
            def _():
                pltpu.make_async_remote_copy(
                    src_ref=source,
                    dst_ref=target,
                    send_sem=g_send_sem,
                    recv_sem=g_recv_sem,
                    device_id=(peer, tp),
                    device_id_type=MESH,
                ).start()

    def step(j, carry):
        @pl.when(j < 8)
        def _():
            stage_terms(j)

        @pl.when((j >= 2) & (j < 10))
        def _():
            stage_y(j - 2)

        @pl.when(j >= 3)
        def _():
            stage_x(j - 3)

        return carry

    lax.fori_loop(0, 11, step, 0)

    def drain(j, carry):
        for d in (1, 2, 3):
            y_copy(j, d).wait_send()
        x_copy(j).wait_send()
        return carry

    lax.fori_loop(0, 8, drain, 0)
    many = gh_ref.at[pl.ds(0, 31 * ROWS)]
    for a in range(3):
        pltpu.make_async_copy(sources[a].at[:, col(0)], targets[a].at[row(0), :], own_sem.at[a]).wait()
        pltpu.make_async_copy(many, many, send_sem.at[a]).wait()
        pltpu.make_async_copy(many, many, recv_sem.at[a]).wait()
    pltpu.make_async_copy(
        g_send.at[0, :, 0:HD], gh_ref.at[row(0), :], g_own_sem
    ).wait()
    pltpu.make_async_copy(many, many, g_send_sem).wait()
    pltpu.make_async_copy(many, many, g_recv_sem).wait()


def gather_in(queries, key_rows, values, upstream, out_weight):
    any_space = pl.BlockSpec(memory_space=pl.ANY)
    return pl.pallas_call(
        gather_in_kernel,
        out_shape=[jax.ShapeDtypeStruct((D, HD), BF16)] * 4,
        in_specs=[any_space] * 5,
        out_specs=[any_space] * 4,
        scratch_shapes=[
            pltpu.VMEM((8 * ROWS, WIDE), BF16),
            pltpu.VMEM((D, WIDE), BF16),
            pltpu.VMEM((8, 8 * ROWS, WIDE), BF16),
            pltpu.VMEM((8, 3, 256, WIDE), BF16),
            pltpu.VMEM((8, ROWS, WIDE), F32),
            pltpu.VMEM((8, ROWS, WIDE), BF16),
            pltpu.VMEM((8, ROWS, WIDE), BF16),
            pltpu.VMEM((8, ROWS, WIDE), BF16),
            pltpu.SemaphoreType.DMA((2,)),
            pltpu.SemaphoreType.DMA((3,)),
            pltpu.SemaphoreType.DMA((3,)),
            pltpu.SemaphoreType.DMA((3,)),
            pltpu.SemaphoreType.DMA((8, 3)),
            pltpu.SemaphoreType.DMA((8, 3)),
            pltpu.SemaphoreType.DMA((8,)),
            pltpu.SemaphoreType.DMA((8,)),
            pltpu.SemaphoreType.DMA,
            pltpu.SemaphoreType.DMA,
            pltpu.SemaphoreType.DMA,
        ],
        compiler_params=pltpu.CompilerParams(
            collective_id=0, has_side_effects=True, vmem_limit_bytes=60 << 20
        ),
        name="gather_in",
    )(queries, key_rows, values, upstream, out_weight)


def attention_kernel(
    blocks_ref, q_ref, k_ref, v_ref, g_ref, o_ref, dq_ref, dk_ref, dv_ref, dk_sum, dv_sum
):
    factor = 1.0 / math.sqrt(HD)
    dk_sum[...] = jnp.zeros_like(dk_sum)
    dv_sum[...] = jnp.zeros_like(dv_sum)

    def one(a):
        listed = [blocks_ref[a, n] for n in range(NB)]
        q = q_ref[a]
        g = g_ref[a]
        k = jnp.concatenate([k_ref[b] for b in listed], axis=0)
        v = jnp.concatenate([v_ref[b] for b in listed], axis=0)
        over_last = (((1,), (1,)), ((), ()))
        over_first = (((0,), (0,)), ((), ()))
        scores = lax.dot_general(q, k, over_last, preferred_element_type=F32) * factor
        shifted = jnp.exp(scores - jnp.max(scores, axis=-1, keepdims=True))
        soft = shifted * (1.0 / jnp.sum(shifted, axis=-1, keepdims=True))
        low = soft.astype(BF16)
        context = jnp.dot(low, v, preferred_element_type=F32).astype(BF16)
        o_ref[a] = context
        delta = jnp.sum(g.astype(F32) * context.astype(F32), axis=-1, keepdims=True)
        dprobs = lax.dot_general(g, v, over_last, preferred_element_type=F32)
        dscores = (soft * (dprobs - delta) * factor).astype(BF16)
        dq_ref[a] = jnp.dot(dscores, k, preferred_element_type=F32).astype(BF16)
        dk = lax.dot_general(dscores, q, over_first, preferred_element_type=F32)
        dv = lax.dot_general(low, g, over_first, preferred_element_type=F32)
        return listed, dk, dv

    def step(i, carry):
        done = [one(i * 4 + n) for n in range(4)]
        for listed, dk, dv in done:
            for n in range(NB):
                dk_sum[listed[n]] += dk[n * BLK : (n + 1) * BLK]
                dv_sum[listed[n]] += dv[n * BLK : (n + 1) * BLK]
        return carry

    lax.fori_loop(0, 16, step, 0)
    dk_ref[...] = dk_sum[...].astype(BF16)
    dv_ref[...] = dv_sum[...].astype(BF16)


def attention(blocks, q, k, v, g):
    count = D // BLK
    tiles = jax.ShapeDtypeStruct((count, BLK, HD), BF16)
    vmem = pl.BlockSpec(memory_space=pltpu.VMEM)
    results = pl.pallas_call(
        attention_kernel,
        out_shape=[tiles] * 4,
        in_specs=[pl.BlockSpec(memory_space=pltpu.SMEM)] + [vmem] * 4,
        out_specs=[vmem] * 4,
        scratch_shapes=[pltpu.VMEM((count, BLK, HD), F32)] * 2,
        compiler_params=pltpu.CompilerParams(vmem_limit_bytes=40 << 20),
        name="attention",
    )(blocks, *[array.reshape(count, BLK, HD) for array in (q, k, v, g)])
    return [array.reshape(D, HD) for array in results]


def spread_out_kernel(
    o_ref, dq_ref, dk_ref, dv_ref, u_ref,
    att_ref, dqt_ref, dkt_ref, dvt_ref, gw_ref,
    u_buf, every, part, c_got, x_send, x_got, keep, z_send, z_got, final,
    load_sem, a_send_sem, a_recv_sem, own_sem, send_sem, recv_sem, att_sem,
    xl_send_sem, xl_recv_sem, y_send_sem, y_recv_sem, r_send_sem, r_recv_sem,
    c_send_sem, c_recv_sem, xh_send_sem, xh_recv_sem, z_send_sem, z_recv_sem,
):
    me = lax.axis_index("seq")
    tp = lax.axis_index("tp")
    x_hi, z, core = me // 16, lax.rem(me // 2, NZ), lax.rem(me, 2)
    y, x_lo = tp // 2, lax.rem(tp, 2)
    load_u = pltpu.make_async_copy(u_ref, u_buf, load_sem)
    load_u.start()
    enter(me, tp)

    mine = every.at[z, row(tp), col(core * 2 + x_hi)]
    pltpu.make_async_copy(o_ref.at[row(me), :], mine, a_recv_sem.at[z]).start()

    def send_attended(step, carry):
        peer = seq_peer(step, me)
        pltpu.make_async_remote_copy(
            src_ref=o_ref.at[row(peer), :],
            dst_ref=mine,
            send_sem=a_send_sem,
            recv_sem=a_recv_sem.at[z],
            device_id=(peer, tp),
            device_id_type=MESH,
        ).start()
        return carry

    lax.fori_loop(1, NSEQ, send_attended, 0)
    sources = (dq_ref, dk_ref, dv_ref)
    targets = (dqt_ref, dkt_ref, dvt_ref)
    for a in range(3):
        pltpu.make_async_copy(
            sources[a].at[row(me), :], targets[a].at[:, col(me)], own_sem.at[a]
        ).start()

        def send_tokens(step, carry, a=a):
            peer = seq_peer(step, me)
            pltpu.make_async_remote_copy(
                src_ref=sources[a].at[row(peer), :],
                dst_ref=targets[a].at[:, col(me)],
                send_sem=send_sem.at[a],
                recv_sem=recv_sem.at[a],
                device_id=(peer, tp),
                device_id_type=MESH,
            ).start()
            return carry

        lax.fori_loop(1, NSEQ, send_tokens, 0)
    load_u.wait()

    def tp_copy(chunk, sequence, target, send, recv):
        here = every.at[chunk, row(sequence), :]
        return pltpu.make_async_remote_copy(
            src_ref=here,
            dst_ref=here,
            send_sem=send,
            recv_sem=recv,
            device_id=(me, target),
            device_id_type=MESH,
        )

    def xl_copy(chunk):
        return tp_copy(chunk, tp, y * 2 + 1 - x_lo, xl_send_sem.at[chunk], xl_recv_sem.at[chunk])

    def y_copy(chunk, direction, slot):
        target = lax.rem(y + (1 if direction == 0 else NY - 1), NY)
        x = x_lo if slot == 0 else 1 - x_lo
        return tp_copy(
            chunk, y * 2 + x, target * 2 + x_lo,
            y_send_sem.at[direction, slot, chunk], y_recv_sem.at[direction, slot, chunk],
        )

    def relay_copy(chunk, direction):
        target = lax.rem(y + (1 if direction == 0 else NY - 1), NY)
        origin = lax.rem(y + (NY - 1 if direction == 0 else 1), NY)
        x = x_lo if direction == 0 else 1 - x_lo
        return tp_copy(
            chunk, origin * 2 + x, target * 2 + x_lo,
            r_send_sem.at[direction, chunk], r_recv_sem.at[direction, chunk],
        )

    def att_copy(chunk, place):
        head = seq_of(place % 2, chunk, place // 2)
        return pltpu.make_async_copy(
            every.at[chunk, row(tp), place * HD : (place + 1) * HD],
            att_ref.at[:, col(head)],
            att_sem,
        )

    def c_copy(chunk):
        return pltpu.make_async_remote_copy(
            src_ref=part.at[chunk, row(1 - core, 256), :],
            dst_ref=c_got.at[chunk],
            send_sem=c_send_sem.at[chunk],
            recv_sem=c_recv_sem.at[chunk],
            device_id=(seq_of(x_hi, z, 1 - core), tp),
            device_id_type=MESH,
        )

    def xh_copy(chunk):
        return pltpu.make_async_remote_copy(
            src_ref=x_send.at[chunk],
            dst_ref=x_got.at[chunk],
            send_sem=xh_send_sem.at[chunk],
            recv_sem=xh_recv_sem.at[chunk],
            device_id=(seq_of(1 - x_hi, z, core), tp),
            device_id_type=MESH,
        )

    def z_copy(chunk):
        return pltpu.make_async_remote_copy(
            src_ref=z_send.at[chunk],
            dst_ref=z_got.at[z],
            send_sem=z_send_sem.at[chunk],
            recv_sem=z_recv_sem,
            device_id=(seq_of(x_hi, chunk, core), tp),
            device_id_type=MESH,
        )

    def stage_attended(chunk):
        here = every.at[chunk, row(tp), :]
        pltpu.make_async_copy(here, here, a_recv_sem.at[chunk]).wait()
        xl_copy(chunk).start()
        y_copy(chunk, 0, 0).start()
        y_copy(chunk, 1, 0).start()
        for place in range(4):
            att_copy(chunk, place).start()

    def stage_neighbour(chunk):
        xl_copy(chunk).wait_recv()
        y_copy(chunk, 0, 1).start()
        y_copy(chunk, 1, 1).start()

    def stage_relay(chunk):
        y_copy(chunk, 0, 0).wait_recv()
        relay_copy(chunk, 0).start()
        y_copy(chunk, 1, 1).wait_recv()
        relay_copy(chunk, 1).start()

    def stage_product(chunk):
        y_copy(chunk, 0, 1).wait_recv()
        y_copy(chunk, 1, 0).wait_recv()
        relay_copy(chunk, 0).wait_recv()
        relay_copy(chunk, 1).wait_recv()
        part[chunk] = lax.dot_general(
            every[chunk], u_buf[...], (((0,), (0,)), ((), ())), preferred_element_type=F32
        ).astype(BF16)
        c_copy(chunk).start()

    def stage_core(chunk):
        c_copy(chunk).wait_recv()

        def total(x):
            here = pl.ds(pl.multiple_of(core * 256 + x * 128, 128), 128)
            there = pl.ds(pl.multiple_of(x * 128, 128), 128)
            return part[chunk, here, :].astype(F32) + c_got[chunk, there, :].astype(F32)

        x_send[chunk] = total(1 - x_hi).astype(BF16)
        xh_copy(chunk).start()
        keep[chunk] = total(x_hi)

    def stage_x(chunk):
        xh_copy(chunk).wait_recv()
        total = keep[chunk] + x_got[chunk].astype(F32)

        @pl.when(chunk == z)
        def _():
            final[...] = total

        @pl.when(chunk != z)
        def _():
            z_send[chunk] = total.astype(BF16)
            z_copy(chunk).start()

    stages = (
        stage_attended, stage_neighbour, stage_relay, stage_product, stage_core, stage_x,
    )

    def step(j, carry):
        for lag, stage in enumerate(stages):

            @pl.when((j >= lag) & (j < lag + NZ))
            def _():
                stage(chunk_at(j - lag, z))

        return carry

    lax.fori_loop(0, NZ + len(stages) - 1, step, 0)

    def drain(chunk, carry):
        xl_copy(chunk).wait_send()
        for direction in range(2):
            for slot in range(2):
                y_copy(chunk, direction, slot).wait_send()
            relay_copy(chunk, direction).wait_send()
        c_copy(chunk).wait_send()
        xh_copy(chunk).wait_send()

        @pl.when(chunk != z)
        def _():
            z_copy(chunk).wait_send()

        return carry

    lax.fori_loop(0, NZ, drain, 0)
    seven = z_got.at[pl.ds(0, NZ - 1)]
    pltpu.make_async_copy(seven, seven, z_recv_sem).wait()

    def add(d, carry):
        final[...] += z_got[lax.rem(z + d, NZ)].astype(F32)
        return carry

    lax.fori_loop(1, NZ, add, 0)
    gw_ref[...] = final[...]
    whole = every.at[0, row(0), :]
    for chunk in range(NZ):
        pltpu.make_async_copy(whole, whole, att_sem).wait()
    many = o_ref.at[pl.ds(0, 31 * ROWS)]
    pltpu.make_async_copy(many, many, a_send_sem).wait()
    for a in range(3):
        pltpu.make_async_copy(sources[a].at[row(0), :], targets[a].at[:, col(0)], own_sem.at[a]).wait()
        pltpu.make_async_copy(many, many, send_sem.at[a]).wait()
        pltpu.make_async_copy(many, many, recv_sem.at[a]).wait()


def spread_out(attended, dq, dk, dv, upstream):
    any_space = pl.BlockSpec(memory_space=pl.ANY)
    dma = pltpu.SemaphoreType.DMA
    tokens = jax.ShapeDtypeStruct((ROWS, D), BF16)
    return pl.pallas_call(
        spread_out_kernel,
        out_shape=[tokens] * 4 + [jax.ShapeDtypeStruct((ROWS, WIDE), F32)],
        in_specs=[any_space] * 5,
        out_specs=[any_space] * 4 + [pl.BlockSpec(memory_space=pltpu.VMEM)],
        scratch_shapes=[
            pltpu.VMEM((8 * ROWS, WIDE), BF16),
            pltpu.VMEM((NZ, 8 * ROWS, WIDE), BF16),
            pltpu.VMEM((NZ, 4 * ROWS, WIDE), BF16),
            pltpu.VMEM((NZ, 2 * ROWS, WIDE), BF16),
            pltpu.VMEM((NZ, ROWS, WIDE), BF16),
            pltpu.VMEM((NZ, ROWS, WIDE), BF16),
            pltpu.VMEM((NZ, ROWS, WIDE), F32),
            pltpu.VMEM((NZ, ROWS, WIDE), BF16),
            pltpu.VMEM((NZ, ROWS, WIDE), BF16),
            pltpu.VMEM((ROWS, WIDE), F32),
            dma, dma, dma((NZ,)), dma((3,)), dma((3,)), dma((3,)), dma,
            dma((NZ,)), dma((NZ,)), dma((2, 2, NZ)), dma((2, 2, NZ)), dma((2, NZ)), dma((2, NZ)),
            dma((NZ,)), dma((NZ,)), dma((NZ,)), dma((NZ,)), dma((NZ,)), dma,
        ],
        compiler_params=pltpu.CompilerParams(
            collective_id=1, has_side_effects=True, vmem_limit_bytes=60 << 20
        ),
        name="spread_out",
    )(attended, dq, dk, dv, upstream)


def on_device(queries, key_rows, values, upstream, out_weight, blocks):
    upstream_rows = upstream.reshape(8 * ROWS, WIDE)
    heads = gather_in(queries[0], key_rows[0], values[0], upstream_rows, out_weight)
    results = attention(blocks, *heads)
    attended, dq, dk, dv, grad_weight = spread_out(*results, upstream_rows)
    return (attended[None], dq[None], dk[None], dv[None], grad_weight)


def solution(mesh):
    in_specs = (
        P("tp", "seq", None),
        P("tp", "seq", None),
        P("tp", "seq", None),
        P(None, "seq", "tp"),
        P(None, "tp"),
        P(),
    )
    out_specs = (
        P("tp", "seq", None),
        P("tp", "seq", None),
        P("tp", "seq", None),
        P("tp", "seq", None),
        P("seq", "tp"),
    )
    return jax.shard_map(
        on_device, mesh=mesh, in_specs=in_specs, out_specs=out_specs, check_vma=False
    )
```

```python
import functools
import math

import jax
import jax.numpy as jnp
from jax import lax
from jax.experimental import pallas as pl
from jax.experimental.pallas import tpu as pltpu
from jax.sharding import PartitionSpec as P

HD = 128
BLK = 64
NB = 4
MESH = pl.DeviceIdType.MESH
BF16 = jnp.bfloat16
F32 = jnp.float32

NZ = 8
NY = 4
NSEQ = 32
ROWS = 128
WIDE = 512
D = 4096


def seq_of(x_hi, z, core):
    return x_hi * 16 + z * 2 + core


def near_far(step, place, count):
    half = (step + 1) // 2
    return lax.rem(jnp.where(lax.rem(step, 2) == 1, place + half, place + count - half), count)


def seq_peer(step, me):
    z = near_far(step // 4, lax.rem(me // 2, NZ), NZ)
    x_hi = lax.rem(me // 16 + lax.rem(step, 2), 2)
    core = lax.rem(lax.rem(me, 2) + lax.rem(step // 2, 2), 2)
    return seq_of(x_hi, z, core)


def col(index):
    return pl.ds(pl.multiple_of(index * HD, HD), HD)


def row(index, size=ROWS):
    return pl.ds(pl.multiple_of(index * size, size), size)


def chunk_at(step, z):
    return near_far(NZ - 1 - step, z, NZ)


def enter(me, tp):
    barrier = pltpu.get_barrier_semaphore()

    def greet_seq(d, carry):
        pl.semaphore_signal(
            barrier, inc=1, device_id=(lax.rem(me + d, NSEQ), tp), device_id_type=MESH
        )
        return carry

    def greet_tp(d, carry):
        pl.semaphore_signal(
            barrier, inc=1, device_id=(me, lax.rem(tp + d, 8)), device_id_type=MESH
        )
        return carry

    lax.fori_loop(1, NSEQ, greet_seq, 0)
    lax.fori_loop(1, 8, greet_tp, 0)
    pl.semaphore_wait(barrier, NSEQ - 1 + 7)


OVER_LAST = (((1,), (1,)), ((), ()))
OVER_FIRST = (((0,), (0,)), ((), ()))
FACTOR = 1.0 / math.sqrt(HD)


def whole_kernel(
    table_ref, q_ref, k_ref, v_ref, u_ref, w_ref,
    att_ref, dqt_ref, dkt_ref, dvt_ref, gw_ref,
    u_buf, w_buf, terms, y_got, keep, x_send, x_got, g_send,
    qh, kh, vh, gh, o_buf, dq_buf, dk_buf, dv_buf, soft_buf, dk_sum, dv_sum, dk_far, dv_far,
    every, c_got, xh_got, z_got, final,
    load_sem, own_sem, send_sem, recv_sem, ty_send_sem, ty_recv_sem, tx_send_sem, tx_recv_sem,
    g_send_sem, g_recv_sem,
    a_send_sem, a_recv_sem, d_own_sem, d_send_sem, d_recv_sem, att_sem,
    xl_send_sem, xl_recv_sem, y_send_sem, y_recv_sem, r_send_sem, r_recv_sem,
    c_send_sem, c_recv_sem, xh_send_sem, xh_recv_sem, z_send_sem, z_recv_sem,
):
    me = lax.axis_index("seq")
    tp = lax.axis_index("tp")
    x_hi, z, core = me // 16, lax.rem(me // 2, NZ), lax.rem(me, 2)
    y, x_lo = tp // 2, lax.rem(tp, 2)
    load_u = pltpu.make_async_copy(u_ref, u_buf, load_sem.at[0])
    load_w = pltpu.make_async_copy(w_ref, w_buf, load_sem.at[1])
    load_u.start()
    load_w.start()
    enter(me, tp)

    def send_heads(a):
        source, target = (q_ref, k_ref, v_ref)[a], (qh, kh, vh)[a]
        place = target.at[pl.ds(2 * me, 2)]
        pltpu.make_async_copy(source.at[:, :, col(me)], place, own_sem.at[a]).start()

        def send(step, carry):
            peer = seq_peer(step, me)
            pltpu.make_async_remote_copy(
                src_ref=source.at[:, :, col(peer)],
                dst_ref=place,
                send_sem=send_sem.at[a],
                recv_sem=recv_sem.at[a],
                device_id=(peer, tp),
                device_id_type=MESH,
            ).start()
            return carry

        lax.fori_loop(1, NSEQ, send, 0)

    def ty_copy(j, d):
        other = lax.rem(y + d, NY)
        return pltpu.make_async_remote_copy(
            src_ref=terms.at[j, row(other, 256), :],
            dst_ref=y_got.at[j, d - 1],
            send_sem=ty_send_sem.at[j, d - 1],
            recv_sem=ty_recv_sem.at[j, d - 1],
            device_id=(me, other * 2 + x_lo),
            device_id_type=MESH,
        )

    def tx_copy(j):
        return pltpu.make_async_remote_copy(
            src_ref=x_send.at[j],
            dst_ref=x_got.at[j],
            send_sem=tx_send_sem.at[j],
            recv_sem=tx_recv_sem.at[j],
            device_id=(me, y * 2 + 1 - x_lo),
            device_id_type=MESH,
        )

    def stage_terms(j):
        chunk = chunk_at(j, z)
        for half in range(2):
            rows = pl.ds(pl.multiple_of(half * 2048 + chunk * 256, 256), 256)
            terms[j, :, half * 256 : (half + 1) * 256] = lax.dot_general(
                u_buf[...], w_buf[rows, :], OVER_LAST, preferred_element_type=F32
            ).astype(BF16)
        for d in (2, 1, 3):
            ty_copy(j, d).start()

    def stage_ty(j):
        for d in (1, 2, 3):
            ty_copy(j, d).wait_recv()

        def total(x):
            rows = pl.ds(pl.multiple_of(y * 256 + x * 128, 128), 128)
            here = pl.ds(pl.multiple_of(x * 128, 128), 128)
            result = terms[j, rows, :].astype(F32)
            for d in range(3):
                result = result + y_got[j, d, here, :].astype(F32)
            return result

        x_send[j] = total(1 - x_lo).astype(BF16)
        tx_copy(j).start()
        keep[j] = total(x_lo)

    def stage_tx(j):
        tx_copy(j).wait_recv()
        g_send[j] = (keep[j] + x_got[j].astype(F32)).astype(BF16)
        chunk = chunk_at(j, z)
        for place in range(4):
            peer = seq_of(place // 2, chunk, place % 2)
            source = g_send.at[j, :, place * HD : (place + 1) * HD]
            target = gh.at[row(me), :]

            @pl.when(peer == me)
            def _():
                pltpu.make_async_copy(source, target, own_sem.at[3]).start()

            @pl.when(peer != me)
            def _():
                pltpu.make_async_remote_copy(
                    src_ref=source,
                    dst_ref=target,
                    send_sem=g_send_sem,
                    recv_sem=g_recv_sem,
                    device_id=(peer, tp),
                    device_id_type=MESH,
                ).start()

    def block_at(n):
        return 2 * seq_peer(n // 2, me) + lax.rem(n, 2)

    def tile(a):
        return pl.ds(pl.multiple_of(a * BLK, BLK), BLK)

    def window(a):
        return (lax.rem(a + 63, 64), a, lax.rem(a + 1, 64))

    def key_set(ref, a):
        return jnp.concatenate([ref[b] for b in window(a) + (table_ref[a],)], axis=0)

    def send_rows(source, target, sem_send, sem_recv, sem_own, i):
        peer = seq_peer(i, me)

        @pl.when(i == 0)
        def _():
            pltpu.make_async_copy(source.at[row(me), :], target, sem_own).start()

        @pl.when(i > 0)
        def _():
            pltpu.make_async_remote_copy(
                src_ref=source.at[row(peer), :],
                dst_ref=target,
                send_sem=sem_send,
                recv_sem=sem_recv,
                device_id=(peer, tp),
                device_id_type=MESH,
            ).start()

    my_place = every.at[z, row(tp), col(core * 2 + x_hi)]

    def forward_one(a):
        k, v = key_set(kh, a), key_set(vh, a)
        scores = lax.dot_general(qh[a], k, OVER_LAST, preferred_element_type=F32) * FACTOR
        shifted = jnp.exp(scores - jnp.max(scores, axis=-1, keepdims=True))
        soft = shifted * (1.0 / jnp.sum(shifted, axis=-1, keepdims=True))
        soft_buf[tile(a), :] = soft
        o_buf[tile(a), :] = jnp.dot(soft.astype(BF16), v, preferred_element_type=F32).astype(BF16)

    def forward_pair(i, carry):
        for m in range(4):
            forward_one(block_at(i * 4 + m))
        for m in range(2):
            send_rows(o_buf, my_place, a_send_sem, a_recv_sem.at[z], a_recv_sem.at[z], i * 2 + m)
        return carry

    def backward_one(a):
        q, g = qh[a], gh[tile(a), :]
        k, v = key_set(kh, a), key_set(vh, a)
        soft = soft_buf[tile(a), :]
        context = o_buf[tile(a), :]
        delta = jnp.sum(g.astype(F32) * context.astype(F32), axis=-1, keepdims=True)
        dprobs = lax.dot_general(g, v, OVER_LAST, preferred_element_type=F32)
        dscores = (soft * (dprobs - delta) * FACTOR).astype(BF16)
        dq_buf[tile(a), :] = jnp.dot(dscores, k, preferred_element_type=F32).astype(BF16)
        dk = lax.dot_general(dscores, q, OVER_FIRST, preferred_element_type=F32)
        dv = lax.dot_general(soft.astype(BF16), g, OVER_FIRST, preferred_element_type=F32)
        return dk, dv

    def backward_pair(i):
        places = [i * 4 + m for m in range(4)]
        done = [backward_one(block_at(n)) for n in places]
        for n, (dk, dv) in zip(places, done):
            near = window(block_at(n))
            for m in range(3):
                dk_sum[tile(near[m]), :] += dk[m * BLK : (m + 1) * BLK]
                dv_sum[tile(near[m]), :] += dv[m * BLK : (m + 1) * BLK]
            dk_far[block_at(n) + 1] = dk[3 * BLK :]
            dv_far[block_at(n) + 1] = dv[3 * BLK :]
        for m in range(2):
            send_rows(
                dq_buf, dqt_ref.at[:, col(me)],
                d_send_sem.at[0], d_recv_sem.at[0], d_own_sem.at[0], i * 2 + m,
            )

    def link_far(a, carry):
        before = table_ref[64 + a]
        dk_far[a + 1] += dk_far[before]
        dv_far[a + 1] += dv_far[before]
        return carry

    def finish_keys(i, carry):
        for m in range(2):
            b = 2 * seq_peer(i, me) + m
            dk_buf[tile(b), :] = (dk_sum[tile(b), :] + dk_far[table_ref[128 + b]]).astype(BF16)
            dv_buf[tile(b), :] = (dv_sum[tile(b), :] + dv_far[table_ref[128 + b]]).astype(BF16)
        for n, (source, target) in enumerate(((dk_buf, dkt_ref), (dv_buf, dvt_ref))):
            send_rows(
                source, target.at[:, col(me)],
                d_send_sem.at[n + 1], d_recv_sem.at[n + 1], d_own_sem.at[n + 1], i,
            )
        return carry

    def tp_copy(chunk, sequence, target, send, recv):
        here = every.at[chunk, row(sequence), :]
        return pltpu.make_async_remote_copy(
            src_ref=here,
            dst_ref=here,
            send_sem=send,
            recv_sem=recv,
            device_id=(me, target),
            device_id_type=MESH,
        )

    def xl_copy(chunk):
        return tp_copy(chunk, tp, y * 2 + 1 - x_lo, xl_send_sem.at[chunk], xl_recv_sem.at[chunk])

    def y_copy(chunk, direction, slot):
        target = lax.rem(y + (1 if direction == 0 else NY - 1), NY)
        x = x_lo if slot == 0 else 1 - x_lo
        return tp_copy(
            chunk, y * 2 + x, target * 2 + x_lo,
            y_send_sem.at[direction, slot, chunk], y_recv_sem.at[direction, slot, chunk],
        )

    def relay_copy(chunk, direction):
        target = lax.rem(y + (1 if direction == 0 else NY - 1), NY)
        origin = lax.rem(y + (NY - 1 if direction == 0 else 1), NY)
        x = x_lo if direction == 0 else 1 - x_lo
        return tp_copy(
            chunk, origin * 2 + x, target * 2 + x_lo,
            r_send_sem.at[direction, chunk], r_recv_sem.at[direction, chunk],
        )

    def att_copy(chunk, place):
        head = seq_of(place % 2, chunk, place // 2)
        return pltpu.make_async_copy(
            every.at[chunk, row(tp), place * HD : (place + 1) * HD],
            att_ref.at[:, col(head)],
            att_sem,
        )

    def c_copy(chunk):
        return pltpu.make_async_remote_copy(
            src_ref=terms.at[chunk, row(1 - core, 256), :],
            dst_ref=c_got.at[chunk],
            send_sem=c_send_sem.at[chunk],
            recv_sem=c_recv_sem.at[chunk],
            device_id=(seq_of(x_hi, z, 1 - core), tp),
            device_id_type=MESH,
        )

    def xh_copy(chunk):
        return pltpu.make_async_remote_copy(
            src_ref=x_send.at[chunk],
            dst_ref=xh_got.at[chunk],
            send_sem=xh_send_sem.at[chunk],
            recv_sem=xh_recv_sem.at[chunk],
            device_id=(seq_of(1 - x_hi, z, core), tp),
            device_id_type=MESH,
        )

    def z_copy(chunk):
        return pltpu.make_async_remote_copy(
            src_ref=g_send.at[chunk],
            dst_ref=z_got.at[z],
            send_sem=z_send_sem.at[chunk],
            recv_sem=z_recv_sem,
            device_id=(seq_of(x_hi, chunk, core), tp),
            device_id_type=MESH,
        )

    def stage_attended(chunk):
        here = every.at[chunk, row(tp), :]
        pltpu.make_async_copy(here, here, a_recv_sem.at[chunk]).wait()
        xl_copy(chunk).start()
        y_copy(chunk, 0, 0).start()
        y_copy(chunk, 1, 0).start()
        for place in range(4):
            att_copy(chunk, place).start()

    def stage_neighbour(chunk):
        xl_copy(chunk).wait_recv()
        y_copy(chunk, 0, 1).start()
        y_copy(chunk, 1, 1).start()

    def stage_relay(chunk):
        y_copy(chunk, 0, 0).wait_recv()
        relay_copy(chunk, 0).start()
        y_copy(chunk, 1, 1).wait_recv()
        relay_copy(chunk, 1).start()

    def stage_product(chunk):
        y_copy(chunk, 0, 1).wait_recv()
        y_copy(chunk, 1, 0).wait_recv()
        relay_copy(chunk, 0).wait_recv()
        relay_copy(chunk, 1).wait_recv()
        terms[chunk, 0:WIDE, :] = lax.dot_general(
            every[chunk], u_buf[...], OVER_FIRST, preferred_element_type=F32
        ).astype(BF16)
        c_copy(chunk).start()

    def stage_core(chunk):
        c_copy(chunk).wait_recv()

        def total(x):
            here = pl.ds(pl.multiple_of(core * 256 + x * 128, 128), 128)
            there = pl.ds(pl.multiple_of(x * 128, 128), 128)
            return terms[chunk, here, :].astype(F32) + c_got[chunk, there, :].astype(F32)

        x_send[chunk] = total(1 - x_hi).astype(BF16)
        xh_copy(chunk).start()
        keep[chunk] = total(x_hi)

    def stage_xh(chunk):
        xh_copy(chunk).wait_recv()
        total = keep[chunk] + xh_got[chunk].astype(F32)

        @pl.when(chunk == z)
        def _():
            final[...] = total

        @pl.when(chunk != z)
        def _():
            g_send[chunk] = total.astype(BF16)
            z_copy(chunk).start()

    def when_in(s, low, high, stage):
        @pl.when((s >= low) & (s < high))
        def _():
            stage(near_far(s, z, NZ))

    send_heads(0)
    load_u.wait()
    load_w.wait()
    stage_terms(0)
    send_heads(1)
    stage_terms(1)
    send_heads(2)
    dk_sum[...] = jnp.zeros_like(dk_sum)
    dv_sum[...] = jnp.zeros_like(dv_sum)
    dk_far[...] = jnp.zeros_like(dk_far)
    dv_far[...] = jnp.zeros_like(dv_far)

    def way_in(j, carry):
        @pl.when(j < 8)
        def _():
            stage_terms(j)

        stage_ty(j - 2)

        @pl.when(j >= 3)
        def _():
            stage_tx(j - 3)

        return carry

    lax.fori_loop(2, 8, way_in, 0)
    stage_tx(5)
    many = o_buf.at[pl.ds(0, 31 * ROWS)]
    for a in range(3):
        source, target = (q_ref, k_ref, v_ref)[a], (qh, kh, vh)[a]
        pltpu.make_async_copy(source.at[:, :, col(0)], target.at[pl.ds(0, 2)], own_sem.at[a]).wait()
        pltpu.make_async_copy(many, many, recv_sem.at[a]).wait()

    def forward_part(part, carry):
        lax.fori_loop(part * 4, part * 4 + 4, forward_pair, 0)

        @pl.when(part == 0)
        def _():
            stage_ty(6)

        @pl.when(part == 1)
        def _():
            stage_tx(6)

        return carry

    lax.fori_loop(0, 4, forward_part, 0)
    stage_ty(7)
    stage_tx(7)
    pltpu.make_async_copy(g_send.at[0, :, 0:HD], gh.at[row(0), :], own_sem.at[3]).wait()
    pltpu.make_async_copy(many, many, g_recv_sem).wait()

    def backward_part(i, carry):
        backward_pair(i)

        @pl.when(lax.rem(i, 2) == 1)
        def _():
            s = i // 2
            stage_attended(near_far(s, z, NZ))
            when_in(s - 1, 0, NZ, stage_neighbour)
            when_in(s - 5, 0, NZ, stage_relay)

        return carry

    lax.fori_loop(0, 16, backward_part, 0)
    lax.fori_loop(0, D // BLK, link_far, 0)
    lax.fori_loop(0, NSEQ, finish_keys, 0)
    stage_neighbour(near_far(NZ - 1, z, NZ))

    def drain_in(j, carry):
        for d in (1, 2, 3):
            ty_copy(j, d).wait_send()
        tx_copy(j).wait_send()
        return carry

    lax.fori_loop(0, 8, drain_in, 0)
    for a in range(3):
        pltpu.make_async_copy(many, many, send_sem.at[a]).wait()
    pltpu.make_async_copy(many, many, g_send_sem).wait()

    def way_out(s, carry):
        when_in(s + 3, 3, NZ, stage_relay)
        when_in(s, 0, NZ, stage_product)
        when_in(s - 1, 0, NZ, stage_core)
        when_in(s - 2, 0, NZ, stage_xh)
        return carry

    lax.fori_loop(0, NZ + 2, way_out, 0)

    def drain_out(chunk, carry):
        xl_copy(chunk).wait_send()
        for direction in range(2):
            for slot in range(2):
                y_copy(chunk, direction, slot).wait_send()
            relay_copy(chunk, direction).wait_send()
        c_copy(chunk).wait_send()
        xh_copy(chunk).wait_send()

        @pl.when(chunk != z)
        def _():
            z_copy(chunk).wait_send()

        return carry

    lax.fori_loop(0, NZ, drain_out, 0)
    seven = z_got.at[pl.ds(0, NZ - 1)]
    pltpu.make_async_copy(seven, seven, z_recv_sem).wait()

    def add(d, carry):
        final[...] += z_got[lax.rem(z + d, NZ)].astype(F32)
        return carry

    lax.fori_loop(1, NZ, add, 0)
    gw_ref[...] = final[...]
    whole = every.at[0, row(0), :]
    for chunk in range(NZ):
        pltpu.make_async_copy(whole, whole, att_sem).wait()
    pltpu.make_async_copy(many, many, a_send_sem).wait()
    for a in range(3):
        target = (dqt_ref, dkt_ref, dvt_ref)[a]
        pltpu.make_async_copy(dq_buf.at[row(0), :], target.at[:, col(0)], d_own_sem.at[a]).wait()
        pltpu.make_async_copy(many, many, d_send_sem.at[a]).wait()
        pltpu.make_async_copy(many, many, d_recv_sem.at[a]).wait()


def whole(table, queries, key_rows, values, upstream, out_weight):
    any_space = pl.BlockSpec(memory_space=pl.ANY)
    dma = pltpu.SemaphoreType.DMA
    tokens = jax.ShapeDtypeStruct((ROWS, D), BF16)
    head = pltpu.VMEM((D, HD), BF16)
    tiles = pltpu.VMEM((D // BLK, BLK, HD), BF16)
    head_sum = pltpu.VMEM((D, HD), F32)
    far_sum = pltpu.VMEM((D // BLK + 1, BLK, HD), F32)
    piece = pltpu.VMEM((NZ, ROWS, WIDE), BF16)
    return pl.pallas_call(
        whole_kernel,
        out_shape=[tokens] * 4 + [jax.ShapeDtypeStruct((ROWS, WIDE), F32)],
        in_specs=[pl.BlockSpec(memory_space=pltpu.SMEM)] + [any_space] * 5,
        out_specs=[any_space] * 4 + [pl.BlockSpec(memory_space=pltpu.VMEM)],
        scratch_shapes=[
            pltpu.VMEM((8 * ROWS, WIDE), BF16),
            pltpu.VMEM((D, WIDE), BF16),
            pltpu.VMEM((8, 8 * ROWS, WIDE), BF16),
            pltpu.VMEM((8, 3, 256, WIDE), BF16),
            pltpu.VMEM((8, ROWS, WIDE), F32),
            piece, piece, piece,
            tiles, tiles, tiles, head, head, head, head, head,
            pltpu.VMEM((D, NB * BLK), F32),
            head_sum, head_sum, far_sum, far_sum,
            pltpu.VMEM((NZ, 8 * ROWS, WIDE), BF16),
            pltpu.VMEM((NZ, 2 * ROWS, WIDE), BF16),
            piece, piece,
            pltpu.VMEM((ROWS, WIDE), F32),
            dma((2,)), dma((4,)), dma((3,)), dma((3,)), dma((8, 3)), dma((8, 3)), dma((8,)), dma((8,)),
            dma, dma,
            dma, dma((NZ,)), dma((3,)), dma((3,)), dma((3,)), dma,
            dma((NZ,)), dma((NZ,)), dma((2, 2, NZ)), dma((2, 2, NZ)), dma((2, NZ)), dma((2, NZ)),
            dma((NZ,)), dma((NZ,)), dma((NZ,)), dma((NZ,)), dma((NZ,)), dma,
        ],
        compiler_params=pltpu.CompilerParams(
            collective_id=0, has_side_effects=True, vmem_limit_bytes=63 << 20
        ),
        name="whole",
    )(table, queries, key_rows, values, upstream, out_weight)


def far_table(blocks):
    count = blocks.shape[0]
    far = blocks[:, NB - 1][None, :]
    across = lax.broadcasted_iota(jnp.int32, (3 * count, count), 1)
    down = lax.broadcasted_iota(jnp.int32, (3 * count, count), 0)
    own = jnp.tile(blocks[:, NB - 1], 3)[:, None]
    kind, place = down // count, down % count
    value = jnp.where(
        kind == 0,
        jnp.where(across == place, far, 0),
        jnp.where(
            kind == 1,
            jnp.where((far == own) & (across < place), across + 1, 0),
            jnp.where(far == place, across + 1, 0),
        ),
    )
    return jnp.max(value, axis=1)


def on_device(queries, key_rows, values, upstream, out_weight, blocks):
    pairs = [array.reshape(2, BLK, D) for array in (queries, key_rows, values)]
    attended, dq, dk, dv, grad_weight = whole(
        far_table(blocks), *pairs, upstream.reshape(8 * ROWS, WIDE), out_weight
    )
    return (attended[None], dq[None], dk[None], dv[None], grad_weight)


def solution(mesh):
    in_specs = (
        P("tp", "seq", None),
        P("tp", "seq", None),
        P("tp", "seq", None),
        P(None, "seq", "tp"),
        P(None, "tp"),
        P(),
    )
    out_specs = (
        P("tp", "seq", None),
        P("tp", "seq", None),
        P("tp", "seq", None),
        P("tp", "seq", None),
        P("seq", "tp"),
    )
    return jax.shard_map(
        on_device, mesh=mesh, in_specs=in_specs, out_specs=out_specs, check_vma=False
    )
```

```python
import functools
import math

import jax
import jax.numpy as jnp
from jax import lax
from jax.experimental import pallas as pl
from jax.experimental.pallas import tpu as pltpu
from jax.sharding import PartitionSpec as P

HD = 128
BLK = 64
NB = 4
MESH = pl.DeviceIdType.MESH
BF16 = jnp.bfloat16
F32 = jnp.float32

NZ = 8
NY = 4
NSEQ = 32
ROWS = 128
WIDE = 512
D = 4096


def seq_of(x_hi, z, core):
    return x_hi * 16 + z * 2 + core


def near_far(step, place, count):
    half = (step + 1) // 2
    return lax.rem(jnp.where(lax.rem(step, 2) == 1, place + half, place + count - half), count)


def seq_peer(step, me):
    z = near_far(step // 4, lax.rem(me // 2, NZ), NZ)
    x_hi = lax.rem(me // 16 + lax.rem(step, 2), 2)
    core = lax.rem(lax.rem(me, 2) + lax.rem(step // 2, 2), 2)
    return seq_of(x_hi, z, core)


def col(index):
    return pl.ds(pl.multiple_of(index * HD, HD), HD)


def row(index, size=ROWS):
    return pl.ds(pl.multiple_of(index * size, size), size)


def chunk_at(step, z):
    return near_far(NZ - 1 - step, z, NZ)


def enter(me, tp):
    barrier = pltpu.get_barrier_semaphore()

    def greet_seq(d, carry):
        pl.semaphore_signal(
            barrier, inc=1, device_id=(lax.rem(me + d, NSEQ), tp), device_id_type=MESH
        )
        return carry

    def greet_tp(d, carry):
        pl.semaphore_signal(
            barrier, inc=1, device_id=(me, lax.rem(tp + d, 8)), device_id_type=MESH
        )
        return carry

    lax.fori_loop(1, NSEQ, greet_seq, 0)
    lax.fori_loop(1, 8, greet_tp, 0)
    pl.semaphore_wait(barrier, NSEQ - 1 + 7)


OVER_LAST = (((1,), (1,)), ((), ()))
OVER_FIRST = (((0,), (0,)), ((), ()))
FACTOR = 1.0 / math.sqrt(HD)


def whole_kernel(
    table_ref, q_ref, k_ref, v_ref, u_ref, w_ref,
    att_ref, dqt_ref, dkt_ref, dvt_ref, gw_ref,
    u_buf, w_buf, terms, y_got, keep, x_send, x_got, g_send,
    qh, kh, vh, gh, o_buf, dq_buf, dk_buf, dv_buf, soft_buf, dk_sum, dv_sum, dk_far, dv_far,
    every, c_got, xh_got, z_got, final,
    load_sem, own_sem, send_sem, recv_sem, ty_send_sem, ty_recv_sem, tx_send_sem, tx_recv_sem,
    g_send_sem, g_recv_sem,
    a_send_sem, a_recv_sem, d_own_sem, d_send_sem, d_recv_sem, att_sem,
    xl_send_sem, xl_recv_sem, y_send_sem, y_recv_sem, r_send_sem, r_recv_sem,
    c_send_sem, c_recv_sem, xh_send_sem, xh_recv_sem, z_send_sem, z_recv_sem,
):
    me = lax.axis_index("seq")
    tp = lax.axis_index("tp")
    x_hi, z, core = me // 16, lax.rem(me // 2, NZ), lax.rem(me, 2)
    y, x_lo = tp // 2, lax.rem(tp, 2)
    load_u = pltpu.make_async_copy(u_ref, u_buf, load_sem.at[0])
    load_w = pltpu.make_async_copy(w_ref, w_buf, load_sem.at[1])
    load_u.start()
    load_w.start()
    enter(me, tp)

    def send_heads(a):
        source, target = (q_ref, k_ref, v_ref)[a], (qh, kh, vh)[a]
        place = target.at[pl.ds(2 * me, 2)]
        pltpu.make_async_copy(source.at[:, :, col(me)], place, own_sem.at[a]).start()

        def send(step, carry):
            peer = seq_peer(step, me)
            pltpu.make_async_remote_copy(
                src_ref=source.at[:, :, col(peer)],
                dst_ref=place,
                send_sem=send_sem.at[a],
                recv_sem=recv_sem.at[a],
                device_id=(peer, tp),
                device_id_type=MESH,
            ).start()
            return carry

        lax.fori_loop(1, NSEQ, send, 0)

    up, down = lax.rem(y + 1, NY), lax.rem(y + NY - 1, NY)
    across = lax.rem(y + 2, NY)

    def term_rows(target, x):
        return pl.ds(pl.multiple_of(target * 256 + x * 128, 128), 128)

    def ty_copy(j, h):
        to = (down, up, up, down, down, up)[h]
        goal = across if h >= 4 else to
        return pltpu.make_async_remote_copy(
            src_ref=terms.at[j, term_rows(goal, h % 2), :],
            dst_ref=y_got.at[j, h],
            send_sem=ty_send_sem.at[j, h],
            recv_sem=ty_recv_sem.at[j, h],
            device_id=(me, to * 2 + x_lo),
            device_id_type=MESH,
        )

    def tx_copy(j):
        return pltpu.make_async_remote_copy(
            src_ref=x_send.at[j],
            dst_ref=x_got.at[j],
            send_sem=tx_send_sem.at[j],
            recv_sem=tx_recv_sem.at[j],
            device_id=(me, y * 2 + 1 - x_lo),
            device_id_type=MESH,
        )

    def stage_terms(j):
        chunk = chunk_at(j, z)
        for half in range(2):
            rows = pl.ds(pl.multiple_of(half * 2048 + chunk * 256, 256), 256)
            terms[j, :, half * 256 : (half + 1) * 256] = lax.dot_general(
                u_buf[...], w_buf[rows, :], OVER_LAST, preferred_element_type=F32
            ).astype(BF16)
        for h in (4, 5, 2, 3):
            ty_copy(j, h).start()

    def stage_second(j):
        for h in (0, 1):
            ty_copy(j, 4 + h).wait_recv()
            rows = term_rows((down, up)[h], h)
            terms[j, rows, :] = (
                terms[j, rows, :].astype(F32) + y_got[j, 4 + h].astype(F32)
            ).astype(BF16)
            ty_copy(j, h).start()

    def stage_ty(j):
        for h in range(4):
            ty_copy(j, h).wait_recv()

        def total(x):
            return (
                terms[j, term_rows(y, x), :].astype(F32)
                + y_got[j, x].astype(F32)
                + y_got[j, 2 + x].astype(F32)
            )

        x_send[j] = total(1 - x_lo).astype(BF16)
        tx_copy(j).start()
        keep[j] = total(x_lo)

    def stage_tx(j):
        tx_copy(j).wait_recv()
        g_send[j] = (keep[j] + x_got[j].astype(F32)).astype(BF16)
        chunk = chunk_at(j, z)
        for place in range(4):
            peer = seq_of(place // 2, chunk, place % 2)
            source = g_send.at[j, :, place * HD : (place + 1) * HD]
            target = gh.at[row(me), :]

            @pl.when(peer == me)
            def _():
                pltpu.make_async_copy(source, target, own_sem.at[3]).start()

            @pl.when(peer != me)
            def _():
                pltpu.make_async_remote_copy(
                    src_ref=source,
                    dst_ref=target,
                    send_sem=g_send_sem,
                    recv_sem=g_recv_sem,
                    device_id=(peer, tp),
                    device_id_type=MESH,
                ).start()

    def block_at(n):
        return 2 * seq_peer(n // 2, me) + lax.rem(n, 2)

    def tile(a):
        return pl.ds(pl.multiple_of(a * BLK, BLK), BLK)

    def window(a):
        return (lax.rem(a + 63, 64), a, lax.rem(a + 1, 64))

    def key_set(ref, a):
        return jnp.concatenate([ref[b] for b in window(a) + (table_ref[a],)], axis=0)

    def send_rows(source, target, sem_send, sem_recv, sem_own, i):
        peer = seq_peer(i, me)

        @pl.when(i == 0)
        def _():
            pltpu.make_async_copy(source.at[row(me), :], target, sem_own).start()

        @pl.when(i > 0)
        def _():
            pltpu.make_async_remote_copy(
                src_ref=source.at[row(peer), :],
                dst_ref=target,
                send_sem=sem_send,
                recv_sem=sem_recv,
                device_id=(peer, tp),
                device_id_type=MESH,
            ).start()

    my_place = every.at[z, row(tp), col(core * 2 + x_hi)]

    def forward_one(a):
        k, v = key_set(kh, a), key_set(vh, a)
        scores = lax.dot_general(qh[a], k, OVER_LAST, preferred_element_type=F32) * FACTOR
        shifted = jnp.exp(scores - jnp.max(scores, axis=-1, keepdims=True))
        soft = shifted * (1.0 / jnp.sum(shifted, axis=-1, keepdims=True))
        soft_buf[tile(a), :] = soft
        o_buf[tile(a), :] = jnp.dot(soft.astype(BF16), v, preferred_element_type=F32).astype(BF16)

    def forward_pair(i, carry):
        for m in range(4):
            forward_one(block_at(i * 4 + m))
        for m in range(2):
            send_rows(o_buf, my_place, a_send_sem, a_recv_sem.at[z], a_recv_sem.at[z], i * 2 + m)
        return carry

    def backward_one(a):
        q, g = qh[a], gh[tile(a), :]
        k, v = key_set(kh, a), key_set(vh, a)
        soft = soft_buf[tile(a), :]
        context = o_buf[tile(a), :]
        delta = jnp.sum(g.astype(F32) * context.astype(F32), axis=-1, keepdims=True)
        dprobs = lax.dot_general(g, v, OVER_LAST, preferred_element_type=F32)
        dscores = (soft * (dprobs - delta) * FACTOR).astype(BF16)
        dq_buf[tile(a), :] = jnp.dot(dscores, k, preferred_element_type=F32).astype(BF16)
        dk = lax.dot_general(dscores, q, OVER_FIRST, preferred_element_type=F32)
        dv = lax.dot_general(soft.astype(BF16), g, OVER_FIRST, preferred_element_type=F32)
        return dk, dv

    def backward_pair(i):
        places = [i * 4 + m for m in range(4)]
        done = [backward_one(block_at(n)) for n in places]
        for n, (dk, dv) in zip(places, done):
            near = window(block_at(n))
            for m in range(3):
                dk_sum[tile(near[m]), :] += dk[m * BLK : (m + 1) * BLK]
                dv_sum[tile(near[m]), :] += dv[m * BLK : (m + 1) * BLK]
            dk_far[block_at(n) + 1] = dk[3 * BLK :]
            dv_far[block_at(n) + 1] = dv[3 * BLK :]
        for m in range(2):
            send_rows(
                dq_buf, dqt_ref.at[:, col(me)],
                d_send_sem.at[0], d_recv_sem.at[0], d_own_sem.at[0], i * 2 + m,
            )

    def link_far(a, carry):
        before = table_ref[64 + a]
        dk_far[a + 1] += dk_far[before]
        dv_far[a + 1] += dv_far[before]
        return carry

    def finish_keys(i, carry):
        for m in range(2):
            b = 2 * seq_peer(i, me) + m
            dk_buf[tile(b), :] = (dk_sum[tile(b), :] + dk_far[table_ref[128 + b]]).astype(BF16)
            dv_buf[tile(b), :] = (dv_sum[tile(b), :] + dv_far[table_ref[128 + b]]).astype(BF16)
        for n, (source, target) in enumerate(((dk_buf, dkt_ref), (dv_buf, dvt_ref))):
            send_rows(
                source, target.at[:, col(me)],
                d_send_sem.at[n + 1], d_recv_sem.at[n + 1], d_own_sem.at[n + 1], i,
            )
        return carry

    def tp_copy(chunk, sequence, target, send, recv):
        here = every.at[chunk, row(sequence), :]
        return pltpu.make_async_remote_copy(
            src_ref=here,
            dst_ref=here,
            send_sem=send,
            recv_sem=recv,
            device_id=(me, target),
            device_id_type=MESH,
        )

    def xl_copy(chunk):
        return tp_copy(chunk, tp, y * 2 + 1 - x_lo, xl_send_sem.at[chunk], xl_recv_sem.at[chunk])

    def y_copy(chunk, direction, slot):
        target = lax.rem(y + (1 if direction == 0 else NY - 1), NY)
        x = x_lo if slot == 0 else 1 - x_lo
        return tp_copy(
            chunk, y * 2 + x, target * 2 + x_lo,
            y_send_sem.at[direction, slot, chunk], y_recv_sem.at[direction, slot, chunk],
        )

    def relay_copy(chunk, direction):
        target = lax.rem(y + (1 if direction == 0 else NY - 1), NY)
        origin = lax.rem(y + (NY - 1 if direction == 0 else 1), NY)
        x = x_lo if direction == 0 else 1 - x_lo
        return tp_copy(
            chunk, origin * 2 + x, target * 2 + x_lo,
            r_send_sem.at[direction, chunk], r_recv_sem.at[direction, chunk],
        )

    def att_copy(chunk, place):
        head = seq_of(place % 2, chunk, place // 2)
        return pltpu.make_async_copy(
            every.at[chunk, row(tp), place * HD : (place + 1) * HD],
            att_ref.at[:, col(head)],
            att_sem,
        )

    def c_copy(chunk):
        return pltpu.make_async_remote_copy(
            src_ref=terms.at[chunk, row(1 - core, 256), :],
            dst_ref=c_got.at[chunk],
            send_sem=c_send_sem.at[chunk],
            recv_sem=c_recv_sem.at[chunk],
            device_id=(seq_of(x_hi, z, 1 - core), tp),
            device_id_type=MESH,
        )

    def xh_copy(chunk):
        return pltpu.make_async_remote_copy(
            src_ref=x_send.at[chunk],
            dst_ref=xh_got.at[chunk],
            send_sem=xh_send_sem.at[chunk],
            recv_sem=xh_recv_sem.at[chunk],
            device_id=(seq_of(1 - x_hi, z, core), tp),
            device_id_type=MESH,
        )

    def z_copy(chunk):
        return pltpu.make_async_remote_copy(
            src_ref=g_send.at[chunk],
            dst_ref=z_got.at[z],
            send_sem=z_send_sem.at[chunk],
            recv_sem=z_recv_sem,
            device_id=(seq_of(x_hi, chunk, core), tp),
            device_id_type=MESH,
        )

    def stage_attended(chunk):
        here = every.at[chunk, row(tp), :]
        pltpu.make_async_copy(here, here, a_recv_sem.at[chunk]).wait()
        xl_copy(chunk).start()
        y_copy(chunk, 0, 0).start()
        y_copy(chunk, 1, 0).start()
        for place in range(4):
            att_copy(chunk, place).start()

    def stage_neighbour(chunk):
        xl_copy(chunk).wait_recv()
        y_copy(chunk, 0, 1).start()
        y_copy(chunk, 1, 1).start()

    def stage_relay(chunk):
        y_copy(chunk, 0, 0).wait_recv()
        relay_copy(chunk, 0).start()
        y_copy(chunk, 1, 1).wait_recv()
        relay_copy(chunk, 1).start()

    def stage_product(chunk):
        y_copy(chunk, 0, 1).wait_recv()
        y_copy(chunk, 1, 0).wait_recv()
        relay_copy(chunk, 0).wait_recv()
        relay_copy(chunk, 1).wait_recv()
        terms[chunk, 0:WIDE, :] = lax.dot_general(
            every[chunk], u_buf[...], OVER_FIRST, preferred_element_type=F32
        ).astype(BF16)
        c_copy(chunk).start()

    def stage_core(chunk):
        c_copy(chunk).wait_recv()

        def total(x):
            here = pl.ds(pl.multiple_of(core * 256 + x * 128, 128), 128)
            there = pl.ds(pl.multiple_of(x * 128, 128), 128)
            return terms[chunk, here, :].astype(F32) + c_got[chunk, there, :].astype(F32)

        x_send[chunk] = total(1 - x_hi).astype(BF16)
        xh_copy(chunk).start()
        keep[chunk] = total(x_hi)

    def stage_xh(chunk):
        xh_copy(chunk).wait_recv()
        total = keep[chunk] + xh_got[chunk].astype(F32)

        @pl.when(chunk == z)
        def _():
            final[...] = total

        @pl.when(chunk != z)
        def _():
            g_send[chunk] = total.astype(BF16)
            z_copy(chunk).start()

    def when_in(s, low, high, stage):
        @pl.when((s >= low) & (s < high))
        def _():
            stage(near_far(s, z, NZ))

    send_heads(0)
    load_u.wait()
    load_w.wait()
    stage_terms(0)
    send_heads(1)
    stage_terms(1)
    send_heads(2)
    stage_second(0)
    dk_sum[...] = jnp.zeros_like(dk_sum)
    dv_sum[...] = jnp.zeros_like(dv_sum)
    dk_far[...] = jnp.zeros_like(dk_far)
    dv_far[...] = jnp.zeros_like(dv_far)

    def way_in(j, carry):
        @pl.when(j < 8)
        def _():
            stage_terms(j)

        @pl.when((j >= 2) & (j <= 8))
        def _():
            stage_second(j - 1)

        @pl.when((j >= 3) & (j < 11))
        def _():
            stage_ty(j - 3)

        @pl.when(j >= 4)
        def _():
            stage_tx(j - 4)

        return carry

    lax.fori_loop(2, 12, way_in, 0)
    many = o_buf.at[pl.ds(0, 31 * ROWS)]
    for a in range(3):
        source, target = (q_ref, k_ref, v_ref)[a], (qh, kh, vh)[a]
        pltpu.make_async_copy(source.at[:, :, col(0)], target.at[pl.ds(0, 2)], own_sem.at[a]).wait()
        pltpu.make_async_copy(many, many, recv_sem.at[a]).wait()

    lax.fori_loop(0, 16, forward_pair, 0)
    pltpu.make_async_copy(g_send.at[0, :, 0:HD], gh.at[row(0), :], own_sem.at[3]).wait()
    pltpu.make_async_copy(many, many, g_recv_sem).wait()

    def backward_part(i, carry):
        backward_pair(i)

        @pl.when(lax.rem(i, 2) == 1)
        def _():
            s = i // 2
            stage_attended(near_far(s, z, NZ))
            when_in(s - 1, 0, NZ, stage_neighbour)
            when_in(s - 5, 0, NZ, stage_relay)

        return carry

    lax.fori_loop(0, 16, backward_part, 0)
    lax.fori_loop(0, D // BLK, link_far, 0)
    lax.fori_loop(0, NSEQ, finish_keys, 0)
    stage_neighbour(near_far(NZ - 1, z, NZ))

    def drain_in(j, carry):
        for h in range(6):
            ty_copy(j, h).wait_send()
        tx_copy(j).wait_send()
        return carry

    lax.fori_loop(0, 8, drain_in, 0)
    for a in range(3):
        pltpu.make_async_copy(many, many, send_sem.at[a]).wait()
    pltpu.make_async_copy(many, many, g_send_sem).wait()

    def way_out(s, carry):
        when_in(s + 3, 3, NZ, stage_relay)
        when_in(s, 0, NZ, stage_product)
        when_in(s - 1, 0, NZ, stage_core)
        when_in(s - 2, 0, NZ, stage_xh)
        return carry

    lax.fori_loop(0, NZ + 2, way_out, 0)

    def drain_out(chunk, carry):
        xl_copy(chunk).wait_send()
        for direction in range(2):
            for slot in range(2):
                y_copy(chunk, direction, slot).wait_send()
            relay_copy(chunk, direction).wait_send()
        c_copy(chunk).wait_send()
        xh_copy(chunk).wait_send()

        @pl.when(chunk != z)
        def _():
            z_copy(chunk).wait_send()

        return carry

    lax.fori_loop(0, NZ, drain_out, 0)
    seven = z_got.at[pl.ds(0, NZ - 1)]
    pltpu.make_async_copy(seven, seven, z_recv_sem).wait()

    def add(d, carry):
        final[...] += z_got[lax.rem(z + d, NZ)].astype(F32)
        return carry

    lax.fori_loop(1, NZ, add, 0)
    gw_ref[...] = final[...]
    whole = every.at[0, row(0), :]
    for chunk in range(NZ):
        pltpu.make_async_copy(whole, whole, att_sem).wait()
    pltpu.make_async_copy(many, many, a_send_sem).wait()
    for a in range(3):
        target = (dqt_ref, dkt_ref, dvt_ref)[a]
        pltpu.make_async_copy(dq_buf.at[row(0), :], target.at[:, col(0)], d_own_sem.at[a]).wait()
        pltpu.make_async_copy(many, many, d_send_sem.at[a]).wait()
        pltpu.make_async_copy(many, many, d_recv_sem.at[a]).wait()


def whole(table, queries, key_rows, values, upstream, out_weight):
    any_space = pl.BlockSpec(memory_space=pl.ANY)
    dma = pltpu.SemaphoreType.DMA
    tokens = jax.ShapeDtypeStruct((ROWS, D), BF16)
    head = pltpu.VMEM((D, HD), BF16)
    tiles = pltpu.VMEM((D // BLK, BLK, HD), BF16)
    head_sum = pltpu.VMEM((D, HD), F32)
    far_sum = pltpu.VMEM((D // BLK + 1, BLK, HD), F32)
    piece = pltpu.VMEM((NZ, ROWS, WIDE), BF16)
    return pl.pallas_call(
        whole_kernel,
        out_shape=[tokens] * 4 + [jax.ShapeDtypeStruct((ROWS, WIDE), F32)],
        in_specs=[pl.BlockSpec(memory_space=pltpu.SMEM)] + [any_space] * 5,
        out_specs=[any_space] * 4 + [pl.BlockSpec(memory_space=pltpu.VMEM)],
        scratch_shapes=[
            pltpu.VMEM((8 * ROWS, WIDE), BF16),
            pltpu.VMEM((D, WIDE), BF16),
            pltpu.VMEM((8, 8 * ROWS, WIDE), BF16),
            pltpu.VMEM((8, 6, ROWS, WIDE), BF16),
            pltpu.VMEM((8, ROWS, WIDE), F32),
            piece, piece, piece,
            tiles, tiles, tiles, head, head, head, head, head,
            pltpu.VMEM((D, NB * BLK), F32),
            head_sum, head_sum, far_sum, far_sum,
            pltpu.VMEM((NZ, 8 * ROWS, WIDE), BF16),
            pltpu.VMEM((NZ, 2 * ROWS, WIDE), BF16),
            piece, piece,
            pltpu.VMEM((ROWS, WIDE), F32),
            dma((2,)), dma((4,)), dma((3,)), dma((3,)), dma((8, 6)), dma((8, 6)), dma((8,)), dma((8,)),
            dma, dma,
            dma, dma((NZ,)), dma((3,)), dma((3,)), dma((3,)), dma,
            dma((NZ,)), dma((NZ,)), dma((2, 2, NZ)), dma((2, 2, NZ)), dma((2, NZ)), dma((2, NZ)),
            dma((NZ,)), dma((NZ,)), dma((NZ,)), dma((NZ,)), dma((NZ,)), dma,
        ],
        compiler_params=pltpu.CompilerParams(
            collective_id=0, has_side_effects=True, vmem_limit_bytes=63 << 20
        ),
        name="whole",
    )(table, queries, key_rows, values, upstream, out_weight)


def far_table(blocks):
    count = blocks.shape[0]
    far = blocks[:, NB - 1][None, :]
    across = lax.broadcasted_iota(jnp.int32, (3 * count, count), 1)
    down = lax.broadcasted_iota(jnp.int32, (3 * count, count), 0)
    own = jnp.tile(blocks[:, NB - 1], 3)[:, None]
    kind, place = down // count, down % count
    value = jnp.where(
        kind == 0,
        jnp.where(across == place, far, 0),
        jnp.where(
            kind == 1,
            jnp.where((far == own) & (across < place), across + 1, 0),
            jnp.where(far == place, across + 1, 0),
        ),
    )
    return jnp.max(value, axis=1)


def on_device(queries, key_rows, values, upstream, out_weight, blocks):
    pairs = [array.reshape(2, BLK, D) for array in (queries, key_rows, values)]
    attended, dq, dk, dv, grad_weight = whole(
        far_table(blocks), *pairs, upstream.reshape(8 * ROWS, WIDE), out_weight
    )
    return (attended[None], dq[None], dk[None], dv[None], grad_weight)


def solution(mesh):
    in_specs = (
        P("tp", "seq", None),
        P("tp", "seq", None),
        P("tp", "seq", None),
        P(None, "seq", "tp"),
        P(None, "tp"),
        P(),
    )
    out_specs = (
        P("tp", "seq", None),
        P("tp", "seq", None),
        P("tp", "seq", None),
        P("tp", "seq", None),
        P("seq", "tp"),
    )
    return jax.shard_map(
        on_device, mesh=mesh, in_specs=in_specs, out_specs=out_specs, check_vma=False
    )
```

```python
import functools
import math

import jax
import jax.numpy as jnp
from jax import lax
from jax.experimental import pallas as pl
from jax.experimental.pallas import tpu as pltpu
from jax.sharding import PartitionSpec as P

HD = 128
BLK = 64
NB = 4
MESH = pl.DeviceIdType.MESH
BF16 = jnp.bfloat16
F32 = jnp.float32

NZ = 8
NY = 4
NSEQ = 32
ROWS = 128
WIDE = 512
D = 4096


def seq_of(x_hi, z, core):
    return x_hi * 16 + z * 2 + core


def near_far(step, place, count):
    half = (step + 1) // 2
    return lax.rem(jnp.where(lax.rem(step, 2) == 1, place + half, place + count - half), count)


def seq_peer(step, me):
    z = near_far(step // 4, lax.rem(me // 2, NZ), NZ)
    x_hi = lax.rem(me // 16 + lax.rem(step, 2), 2)
    core = lax.rem(lax.rem(me, 2) + lax.rem(step // 2, 2), 2)
    return seq_of(x_hi, z, core)


def col(index):
    return pl.ds(pl.multiple_of(index * HD, HD), HD)


def row(index, size=ROWS):
    return pl.ds(pl.multiple_of(index * size, size), size)


def chunk_at(step, z):
    return near_far(NZ - 1 - step, z, NZ)


def enter(me, tp):
    barrier = pltpu.get_barrier_semaphore()

    def greet_seq(d, carry):
        pl.semaphore_signal(
            barrier, inc=1, device_id=(lax.rem(me + d, NSEQ), tp), device_id_type=MESH
        )
        return carry

    def greet_tp(d, carry):
        pl.semaphore_signal(
            barrier, inc=1, device_id=(me, lax.rem(tp + d, 8)), device_id_type=MESH
        )
        return carry

    lax.fori_loop(1, NSEQ, greet_seq, 0)
    lax.fori_loop(1, 8, greet_tp, 0)
    pl.semaphore_wait(barrier, NSEQ - 1 + 7)


OVER_LAST = (((1,), (1,)), ((), ()))
OVER_FIRST = (((0,), (0,)), ((), ()))
FACTOR = 1.0 / math.sqrt(HD)


def whole_kernel(
    table_ref, q_ref, k_ref, v_ref, u_ref, w_ref,
    att_ref, dqt_ref, dkt_ref, dvt_ref, gw_ref,
    u_buf, w_buf, terms, y_got, keep, x_send, x_got, g_send,
    qh, kh, vh, gh, o_buf, dq_buf, dk_buf, dv_buf, soft_buf, dk_sum, dv_sum, dk_far, dv_far,
    every, c_got, xh_got, z_got,
    load_sem, own_sem, send_sem, recv_sem, ty_send_sem, ty_recv_sem, tx_send_sem, tx_recv_sem,
    g_send_sem, g_recv_sem,
    a_send_sem, a_recv_sem, d_own_sem, d_send_sem, d_recv_sem, att_sem,
    xl_send_sem, xl_recv_sem, y_send_sem, y_recv_sem, r_send_sem, r_recv_sem,
    c_send_sem, c_recv_sem, xh_send_sem, xh_recv_sem, z_send_sem, z_recv_sem,
):
    me = lax.axis_index("seq")
    tp = lax.axis_index("tp")
    x_hi, z, core = me // 16, lax.rem(me // 2, NZ), lax.rem(me, 2)
    y, x_lo = tp // 2, lax.rem(tp, 2)
    load_u = pltpu.make_async_copy(u_ref, u_buf, load_sem.at[0])
    load_w = pltpu.make_async_copy(w_ref, w_buf, load_sem.at[1])
    load_u.start()
    load_w.start()
    enter(me, tp)

    def send_heads(a):
        source, target = (q_ref, k_ref, v_ref)[a], (qh, kh, vh)[a]
        place = target.at[pl.ds(2 * me, 2)]
        pltpu.make_async_copy(source.at[:, :, col(me)], place, own_sem.at[a]).start()

        def send(step, carry):
            peer = seq_peer(step, me)
            pltpu.make_async_remote_copy(
                src_ref=source.at[:, :, col(peer)],
                dst_ref=place,
                send_sem=send_sem.at[a],
                recv_sem=recv_sem.at[a],
                device_id=(peer, tp),
                device_id_type=MESH,
            ).start()
            return carry

        lax.fori_loop(1, NSEQ, send, 0)

    up, down = lax.rem(y + 1, NY), lax.rem(y + NY - 1, NY)
    across = lax.rem(y + 2, NY)

    def term_rows(target, x):
        return pl.ds(pl.multiple_of(target * 256 + x * 128, 128), 128)

    def ty_copy(j, h):
        to = (down, up, up, down, down, up)[h]
        goal = across if h >= 4 else to
        return pltpu.make_async_remote_copy(
            src_ref=terms.at[j, term_rows(goal, h % 2), :],
            dst_ref=y_got.at[j, h],
            send_sem=ty_send_sem.at[j, h],
            recv_sem=ty_recv_sem.at[j, h],
            device_id=(me, to * 2 + x_lo),
            device_id_type=MESH,
        )

    def tx_copy(j):
        return pltpu.make_async_remote_copy(
            src_ref=x_send.at[j],
            dst_ref=x_got.at[j],
            send_sem=tx_send_sem.at[j],
            recv_sem=tx_recv_sem.at[j],
            device_id=(me, y * 2 + 1 - x_lo),
            device_id_type=MESH,
        )

    def stage_terms(j):
        chunk = chunk_at(j, z)
        for half in range(2):
            rows = pl.ds(pl.multiple_of(half * 2048 + chunk * 256, 256), 256)
            terms[j, :, half * 256 : (half + 1) * 256] = lax.dot_general(
                u_buf[...], w_buf[rows, :], OVER_LAST, preferred_element_type=F32
            ).astype(BF16)
        for h in (4, 5, 2, 3):
            ty_copy(j, h).start()

    def stage_second(j):
        for h in (0, 1):
            ty_copy(j, 4 + h).wait_recv()
            rows = term_rows((down, up)[h], h)
            terms[j, rows, :] = (
                terms[j, rows, :].astype(F32) + y_got[j, 4 + h].astype(F32)
            ).astype(BF16)
            ty_copy(j, h).start()

    def stage_ty(j):
        for h in range(4):
            ty_copy(j, h).wait_recv()

        def total(x):
            return (
                terms[j, term_rows(y, x), :].astype(F32)
                + y_got[j, x].astype(F32)
                + y_got[j, 2 + x].astype(F32)
            )

        x_send[j] = total(1 - x_lo).astype(BF16)
        tx_copy(j).start()
        keep[j] = total(x_lo)

    def stage_tx(j):
        tx_copy(j).wait_recv()
        g_send[j] = (keep[j] + x_got[j].astype(F32)).astype(BF16)
        chunk = chunk_at(j, z)
        for place in range(4):
            peer = seq_of(place // 2, chunk, place % 2)
            source = g_send.at[j, :, place * HD : (place + 1) * HD]
            target = gh.at[row(me), :]

            @pl.when(peer == me)
            def _():
                pltpu.make_async_copy(source, target, own_sem.at[3]).start()

            @pl.when(peer != me)
            def _():
                pltpu.make_async_remote_copy(
                    src_ref=source,
                    dst_ref=target,
                    send_sem=g_send_sem,
                    recv_sem=g_recv_sem,
                    device_id=(peer, tp),
                    device_id_type=MESH,
                ).start()

    def visit(i):
        return seq_peer(NSEQ - 1 - i, me)

    def block_at(n):
        return 2 * visit(n // 2) + lax.rem(n, 2)

    def tile(a):
        return pl.ds(pl.multiple_of(a * BLK, BLK), BLK)

    def window(a):
        return (lax.rem(a + 63, 64), a, lax.rem(a + 1, 64))

    def key_set(ref, a):
        return jnp.concatenate([ref[b] for b in window(a) + (table_ref[a],)], axis=0)

    def send_rows(source, target, sem_send, sem_recv, sem_own, i):
        peer = visit(i)

        @pl.when(i == NSEQ - 1)
        def _():
            pltpu.make_async_copy(source.at[row(me), :], target, sem_own).start()

        @pl.when(i < NSEQ - 1)
        def _():
            pltpu.make_async_remote_copy(
                src_ref=source.at[row(peer), :],
                dst_ref=target,
                send_sem=sem_send,
                recv_sem=sem_recv,
                device_id=(peer, tp),
                device_id_type=MESH,
            ).start()

    my_place = every.at[z, row(tp), col(core * 2 + x_hi)]

    def forward_one(a):
        k, v = key_set(kh, a), key_set(vh, a)
        scores = lax.dot_general(qh[a], k, OVER_LAST, preferred_element_type=F32) * FACTOR
        shifted = jnp.exp(scores - jnp.max(scores, axis=-1, keepdims=True))
        soft = shifted * (1.0 / jnp.sum(shifted, axis=-1, keepdims=True))
        soft_buf[tile(a), :] = soft
        o_buf[tile(a), :] = jnp.dot(soft.astype(BF16), v, preferred_element_type=F32).astype(BF16)

    def forward_pair(i, carry):
        for m in range(4):
            forward_one(block_at(i * 4 + m))
        for m in range(2):
            send_rows(o_buf, my_place, a_send_sem, a_recv_sem.at[z], a_recv_sem.at[z], i * 2 + m)
        return carry

    def backward_one(a):
        q, g = qh[a], gh[tile(a), :]
        k, v = key_set(kh, a), key_set(vh, a)
        soft = soft_buf[tile(a), :]
        context = o_buf[tile(a), :]
        delta = jnp.sum(g.astype(F32) * context.astype(F32), axis=-1, keepdims=True)
        dprobs = lax.dot_general(g, v, OVER_LAST, preferred_element_type=F32)
        dscores = (soft * (dprobs - delta) * FACTOR).astype(BF16)
        dq_buf[tile(a), :] = jnp.dot(dscores, k, preferred_element_type=F32).astype(BF16)
        dk = lax.dot_general(dscores, q, OVER_FIRST, preferred_element_type=F32)
        dv = lax.dot_general(soft.astype(BF16), g, OVER_FIRST, preferred_element_type=F32)
        return dk, dv

    def backward_pair(i):
        places = [i * 4 + m for m in range(4)]
        done = [backward_one(block_at(n)) for n in places]
        for n, (dk, dv) in zip(places, done):
            near = window(block_at(n))
            for m in range(3):
                dk_sum[tile(near[m]), :] += dk[m * BLK : (m + 1) * BLK]
                dv_sum[tile(near[m]), :] += dv[m * BLK : (m + 1) * BLK]
            dk_far[block_at(n) + 1] = dk[3 * BLK :]
            dv_far[block_at(n) + 1] = dv[3 * BLK :]
        for m in range(2):
            send_rows(
                dq_buf, dqt_ref.at[:, col(me)],
                d_send_sem.at[0], d_recv_sem.at[0], d_own_sem.at[0], i * 2 + m,
            )

    def link_far(a, carry):
        before = table_ref[64 + a]
        dk_far[a + 1] += dk_far[before]
        dv_far[a + 1] += dv_far[before]
        return carry

    def finish_keys(i, carry):
        for m in range(2):
            b = 2 * visit(i) + m
            dk_buf[tile(b), :] = (dk_sum[tile(b), :] + dk_far[table_ref[128 + b]]).astype(BF16)
            dv_buf[tile(b), :] = (dv_sum[tile(b), :] + dv_far[table_ref[128 + b]]).astype(BF16)
        for n, (source, target) in enumerate(((dk_buf, dkt_ref), (dv_buf, dvt_ref))):
            send_rows(
                source, target.at[:, col(me)],
                d_send_sem.at[n + 1], d_recv_sem.at[n + 1], d_own_sem.at[n + 1], i,
            )
        return carry

    def tp_copy(chunk, sequence, target, send, recv):
        here = every.at[chunk, row(sequence), :]
        return pltpu.make_async_remote_copy(
            src_ref=here,
            dst_ref=here,
            send_sem=send,
            recv_sem=recv,
            device_id=(me, target),
            device_id_type=MESH,
        )

    def xl_copy(chunk):
        return tp_copy(chunk, tp, y * 2 + 1 - x_lo, xl_send_sem.at[chunk], xl_recv_sem.at[chunk])

    def y_copy(chunk, direction, slot):
        target = lax.rem(y + (1 if direction == 0 else NY - 1), NY)
        x = x_lo if slot == 0 else 1 - x_lo
        return tp_copy(
            chunk, y * 2 + x, target * 2 + x_lo,
            y_send_sem.at[direction, slot, chunk], y_recv_sem.at[direction, slot, chunk],
        )

    def relay_copy(chunk, direction):
        target = lax.rem(y + (1 if direction == 0 else NY - 1), NY)
        origin = lax.rem(y + (NY - 1 if direction == 0 else 1), NY)
        x = x_lo if direction == 0 else 1 - x_lo
        return tp_copy(
            chunk, origin * 2 + x, target * 2 + x_lo,
            r_send_sem.at[direction, chunk], r_recv_sem.at[direction, chunk],
        )

    def att_copy(chunk, place):
        head = seq_of(place % 2, chunk, place // 2)
        return pltpu.make_async_copy(
            every.at[chunk, row(tp), place * HD : (place + 1) * HD],
            att_ref.at[:, col(head)],
            att_sem,
        )

    def c_copy(chunk):
        return pltpu.make_async_remote_copy(
            src_ref=terms.at[chunk, row(1 - core, 256), :],
            dst_ref=c_got.at[chunk],
            send_sem=c_send_sem.at[chunk],
            recv_sem=c_recv_sem.at[chunk],
            device_id=(seq_of(x_hi, z, 1 - core), tp),
            device_id_type=MESH,
        )

    def xh_copy(chunk):
        return pltpu.make_async_remote_copy(
            src_ref=x_send.at[chunk],
            dst_ref=xh_got.at[chunk],
            send_sem=xh_send_sem.at[chunk],
            recv_sem=xh_recv_sem.at[chunk],
            device_id=(seq_of(1 - x_hi, z, core), tp),
            device_id_type=MESH,
        )

    def steps_up(chunk):
        return lax.rem(chunk + NZ - z, NZ)

    def z_copy(chunk):
        t = steps_up(chunk)
        goes_up = (t < 4) | ((t == 4) & (core == 0))
        target = lax.rem(jnp.where(goes_up, z + 1, z + NZ - 1), NZ)
        slot = jnp.where((target == chunk) & jnp.logical_not(goes_up), NZ, chunk)
        return pltpu.make_async_remote_copy(
            src_ref=g_send.at[chunk],
            dst_ref=z_got.at[slot],
            send_sem=z_send_sem.at[chunk],
            recv_sem=z_recv_sem.at[slot],
            device_id=(seq_of(x_hi, target, core), tp),
            device_id_type=MESH,
        )

    def z_wait(slot):
        pltpu.make_async_copy(z_got.at[slot], z_got.at[slot], z_recv_sem.at[slot]).wait()

    def stage_attended(chunk):
        here = every.at[chunk, row(tp), :]
        pltpu.make_async_copy(here, here, a_recv_sem.at[chunk]).wait()
        xl_copy(chunk).start()
        y_copy(chunk, 0, 0).start()
        y_copy(chunk, 1, 0).start()
        for place in range(4):
            att_copy(chunk, place).start()

    def stage_neighbour(chunk):
        xl_copy(chunk).wait_recv()
        y_copy(chunk, 0, 1).start()
        y_copy(chunk, 1, 1).start()

    def stage_relay(chunk):
        y_copy(chunk, 0, 0).wait_recv()
        relay_copy(chunk, 0).start()
        y_copy(chunk, 1, 1).wait_recv()
        relay_copy(chunk, 1).start()

    def stage_product(chunk):
        y_copy(chunk, 0, 1).wait_recv()
        y_copy(chunk, 1, 0).wait_recv()
        relay_copy(chunk, 0).wait_recv()
        relay_copy(chunk, 1).wait_recv()
        terms[chunk, 0:WIDE, :] = lax.dot_general(
            every[chunk], u_buf[...], OVER_FIRST, preferred_element_type=F32
        ).astype(BF16)
        c_copy(chunk).start()

    def stage_core(chunk):
        c_copy(chunk).wait_recv()

        def total(x):
            here = pl.ds(pl.multiple_of(core * 256 + x * 128, 128), 128)
            there = pl.ds(pl.multiple_of(x * 128, 128), 128)
            return terms[chunk, here, :].astype(F32) + c_got[chunk, there, :].astype(F32)

        x_send[chunk] = total(1 - x_hi).astype(BF16)
        xh_copy(chunk).start()
        keep[chunk] = total(x_hi)

    def stage_xh(chunk):
        xh_copy(chunk).wait_recv()
        t = steps_up(chunk)
        more = (
            (t == 1) | (t == 2) | (t == 6) | (t == 7)
            | ((t == 3) & (core == 0)) | ((t == 5) & (core == 1))
        )
        keep[chunk] += xh_got[chunk].astype(F32)

        @pl.when(t == 0)
        def _():
            z_wait(chunk)
            z_wait(NZ)
            gw_ref[...] = keep[chunk] + z_got[chunk].astype(F32) + z_got[NZ].astype(F32)

        @pl.when(more)
        def _():
            z_wait(chunk)
            keep[chunk] += z_got[chunk].astype(F32)

        @pl.when(t != 0)
        def _():
            g_send[chunk] = keep[chunk].astype(BF16)
            z_copy(chunk).start()

    def when_in(s, low, high, stage):
        @pl.when((s >= low) & (s < high))
        def _():
            stage(chunk_at(s, z))

    send_heads(0)
    load_u.wait()
    load_w.wait()
    stage_terms(0)
    send_heads(1)
    stage_terms(1)
    send_heads(2)
    stage_second(0)
    dk_sum[...] = jnp.zeros_like(dk_sum)
    dv_sum[...] = jnp.zeros_like(dv_sum)
    dk_far[...] = jnp.zeros_like(dk_far)
    dv_far[...] = jnp.zeros_like(dv_far)

    def way_in(j, carry):
        @pl.when(j < 8)
        def _():
            stage_terms(j)

        @pl.when((j >= 2) & (j <= 8))
        def _():
            stage_second(j - 1)

        @pl.when((j >= 3) & (j < 11))
        def _():
            stage_ty(j - 3)

        @pl.when(j >= 4)
        def _():
            stage_tx(j - 4)

        return carry

    lax.fori_loop(2, 12, way_in, 0)
    many = o_buf.at[pl.ds(0, 31 * ROWS)]
    for a in range(3):
        source, target = (q_ref, k_ref, v_ref)[a], (qh, kh, vh)[a]
        pltpu.make_async_copy(source.at[:, :, col(0)], target.at[pl.ds(0, 2)], own_sem.at[a]).wait()
        pltpu.make_async_copy(many, many, recv_sem.at[a]).wait()

    lax.fori_loop(0, 16, forward_pair, 0)
    pltpu.make_async_copy(g_send.at[0, :, 0:HD], gh.at[row(0), :], own_sem.at[3]).wait()
    pltpu.make_async_copy(many, many, g_recv_sem).wait()

    def backward_part(i, carry):
        backward_pair(i)

        @pl.when(lax.rem(i, 2) == 1)
        def _():
            s = i // 2
            stage_attended(chunk_at(s, z))
            when_in(s - 1, 0, NZ, stage_neighbour)
            when_in(s - 5, 0, NZ, stage_relay)

        return carry

    lax.fori_loop(0, 16, backward_part, 0)
    lax.fori_loop(0, D // BLK, link_far, 0)
    lax.fori_loop(0, NSEQ, finish_keys, 0)
    stage_neighbour(chunk_at(NZ - 1, z))

    def drain_in(j, carry):
        for h in range(6):
            ty_copy(j, h).wait_send()
        tx_copy(j).wait_send()
        return carry

    lax.fori_loop(0, 8, drain_in, 0)
    for a in range(3):
        pltpu.make_async_copy(many, many, send_sem.at[a]).wait()
    pltpu.make_async_copy(many, many, g_send_sem).wait()

    def way_out(s, carry):
        when_in(s + 3, 3, NZ, stage_relay)
        when_in(s, 0, NZ, stage_product)
        when_in(s - 1, 0, NZ, stage_core)
        when_in(s - 2, 0, NZ, stage_xh)
        return carry

    lax.fori_loop(0, NZ + 2, way_out, 0)

    def drain_out(chunk, carry):
        xl_copy(chunk).wait_send()
        for direction in range(2):
            for slot in range(2):
                y_copy(chunk, direction, slot).wait_send()
            relay_copy(chunk, direction).wait_send()
        c_copy(chunk).wait_send()
        xh_copy(chunk).wait_send()

        @pl.when(chunk != z)
        def _():
            z_copy(chunk).wait_send()

        return carry

    lax.fori_loop(0, NZ, drain_out, 0)
    whole = every.at[0, row(0), :]
    for chunk in range(NZ):
        pltpu.make_async_copy(whole, whole, att_sem).wait()
    pltpu.make_async_copy(many, many, a_send_sem).wait()
    for a in range(3):
        target = (dqt_ref, dkt_ref, dvt_ref)[a]
        pltpu.make_async_copy(dq_buf.at[row(0), :], target.at[:, col(0)], d_own_sem.at[a]).wait()
        pltpu.make_async_copy(many, many, d_send_sem.at[a]).wait()
        pltpu.make_async_copy(many, many, d_recv_sem.at[a]).wait()


def whole(table, queries, key_rows, values, upstream, out_weight):
    any_space = pl.BlockSpec(memory_space=pl.ANY)
    dma = pltpu.SemaphoreType.DMA
    tokens = jax.ShapeDtypeStruct((ROWS, D), BF16)
    head = pltpu.VMEM((D, HD), BF16)
    tiles = pltpu.VMEM((D // BLK, BLK, HD), BF16)
    head_sum = pltpu.VMEM((D, HD), F32)
    far_sum = pltpu.VMEM((D // BLK + 1, BLK, HD), F32)
    piece = pltpu.VMEM((NZ, ROWS, WIDE), BF16)
    return pl.pallas_call(
        whole_kernel,
        out_shape=[tokens] * 4 + [jax.ShapeDtypeStruct((ROWS, WIDE), F32)],
        in_specs=[pl.BlockSpec(memory_space=pltpu.SMEM)] + [any_space] * 5,
        out_specs=[any_space] * 4 + [pl.BlockSpec(memory_space=pltpu.VMEM)],
        scratch_shapes=[
            pltpu.VMEM((8 * ROWS, WIDE), BF16),
            pltpu.VMEM((D, WIDE), BF16),
            pltpu.VMEM((8, 8 * ROWS, WIDE), BF16),
            pltpu.VMEM((8, 6, ROWS, WIDE), BF16),
            pltpu.VMEM((8, ROWS, WIDE), F32),
            piece, piece, piece,
            tiles, tiles, tiles, head, head, head, head, head,
            pltpu.VMEM((D, NB * BLK), F32),
            head_sum, head_sum, far_sum, far_sum,
            pltpu.VMEM((NZ, 8 * ROWS, WIDE), BF16),
            pltpu.VMEM((NZ, 2 * ROWS, WIDE), BF16),
            piece, pltpu.VMEM((NZ + 1, ROWS, WIDE), BF16),
            dma((2,)), dma((4,)), dma((3,)), dma((3,)), dma((8, 6)), dma((8, 6)), dma((8,)), dma((8,)),
            dma, dma,
            dma, dma((NZ,)), dma((3,)), dma((3,)), dma((3,)), dma,
            dma((NZ,)), dma((NZ,)), dma((2, 2, NZ)), dma((2, 2, NZ)), dma((2, NZ)), dma((2, NZ)),
            dma((NZ,)), dma((NZ,)), dma((NZ,)), dma((NZ,)), dma((NZ,)), dma((NZ + 1,)),
        ],
        compiler_params=pltpu.CompilerParams(
            collective_id=0, has_side_effects=True, vmem_limit_bytes=63 << 20
        ),
        name="whole",
    )(table, queries, key_rows, values, upstream, out_weight)


def far_table(blocks):
    count = blocks.shape[0]
    far = blocks[:, NB - 1][None, :]
    across = lax.broadcasted_iota(jnp.int32, (3 * count, count), 1)
    down = lax.broadcasted_iota(jnp.int32, (3 * count, count), 0)
    own = jnp.tile(blocks[:, NB - 1], 3)[:, None]
    kind, place = down // count, down % count
    value = jnp.where(
        kind == 0,
        jnp.where(across == place, far, 0),
        jnp.where(
            kind == 1,
            jnp.where((far == own) & (across < place), across + 1, 0),
            jnp.where(far == place, across + 1, 0),
        ),
    )
    return jnp.max(value, axis=1)


def on_device(queries, key_rows, values, upstream, out_weight, blocks):
    pairs = [array.reshape(2, BLK, D) for array in (queries, key_rows, values)]
    attended, dq, dk, dv, grad_weight = whole(
        far_table(blocks), *pairs, upstream.reshape(8 * ROWS, WIDE), out_weight
    )
    return (attended[None], dq[None], dk[None], dv[None], grad_weight)


def solution(mesh):
    in_specs = (
        P("tp", "seq", None),
        P("tp", "seq", None),
        P("tp", "seq", None),
        P(None, "seq", "tp"),
        P(None, "tp"),
        P(),
    )
    out_specs = (
        P("tp", "seq", None),
        P("tp", "seq", None),
        P("tp", "seq", None),
        P("tp", "seq", None),
        P("seq", "tp"),
    )
    return jax.shard_map(
        on_device, mesh=mesh, in_specs=in_specs, out_specs=out_specs, check_vma=False
    )
```
